512 devices in a mesh: sensor: 64 (over x, z), tm: 8 (over y, core).
Axes of the slice: x: 4, y: 4, z: 16, core: 2. Of those that a mesh axis runs over, the one named last changes fastest.
Arguments:
- inputs: bfloat16 [4096, 128, 128], P('sensor', 'tm'), may hold values from -6 to 6
- mask: int32 [4096, 128], P('sensor', 'tm'), may hold values 0 or 1
- projector: float32 [64, 128], replicated, may hold values from -6 to 6
- w_key: bfloat16 [128, 128], replicated, may hold values from -0.5 to 0.5
- w_value: bfloat16 [128, 128], replicated, may hold values from -0.5 to 0.5
- w_query: bfloat16 [128, 128], replicated, may hold values from -0.5 to 0.5
- w_out: bfloat16 [128, 128], replicated, may hold values from -0.5 to 0.5
- cotangent: bfloat16 [4096, 128, 128], P('sensor', 'tm'), may hold values from -6 to 6
Outputs:
- layer_out: bfloat16 [4096, 128, 128], P('sensor', 'tm')
- grad_inputs: bfloat16 [4096, 128, 128], P('sensor', 'tm')
- grad_projector: float32 [64, 128], P('tm')
- grad_key: float32 [128, 128], P('tm')
- grad_value: float32 [128, 128], P('tm')
- grad_query: float32 [128, 128], P('tm')
- grad_out: float32 [128, 128], P('tm')
The draws below stay inside these ranges and needn't reach their ends.
All inputs are finite; a program needn't handle non-finite values. No bound on the sum of `mask` on one device may be relied on, other than what follows from the above.
Results may differ from the reference program's by a relative error of at most 0.0095.
Values sent between devices are 32-bit elements; how exact they have to be, the bound alone decides.
A program may use at most 64 MiB of HBM per device.

```python
import jax
import jax.numpy as jnp
from jax import lax

D = 128
K = 64
SENSORS = 4096
STEPS = 128


def touch_ends(values, own_key, least, top_value):
    longest = values.shape.index(max(values.shape))
    spots = []
    for shift in (0, 1):
        where = [jax.random.randint(jax.random.fold_in(own_key, axis), (), 0, length) for axis, length in enumerate(values.shape)]
        where[longest] = (where[longest] + shift) % values.shape[longest]
        spots.append(tuple(where))
    return values.at[spots[0]].set(least).at[spots[1]].set(top_value)


def steps_of(own_key, extent, split, least, top_value):
    gain, own = 1.0, jax.random.fold_in(own_key, 6)
    for position, parts in split:
        heights = jnp.exp(jax.random.uniform(jax.random.fold_in(own, position), (parts,), jnp.float32, least / len(split), top_value / len(split)))
        gain = gain * jnp.repeat(heights, extent[position] // parts).reshape([-1 if axis == position else 1 for axis in range(len(extent))])
    return gain


def noise(rng, shape, deviation, limit, pieces=(), kind=jnp.bfloat16):
    drawn = deviation * jax.random.normal(rng, shape, jnp.float32)
    if pieces:
        drawn = drawn * steps_of(rng, shape, pieces, -0.22, 0.18)
    return jnp.clip(drawn, -limit, limit).astype(kind)


def setup_inputs(seed: int = 0) -> dict:
    keys = jax.random.split(jax.random.key(seed), 9)
    inputs = noise(keys[0], (SENSORS, STEPS, D), 1.0, 6.0, ((0, 64), (1, 8)))
    mask = touch_ends((jax.random.randint(keys[1], (SENSORS, STEPS), 0, 4) < 3).astype(jnp.int32), jax.random.fold_in(keys[1], 1), 0, 1)
    projector = noise(keys[2], (K, D), 1.0, 6.0, (), jnp.float32)
    w_key = noise(keys[3], (D, D), D ** -0.5, 0.5)
    w_value = noise(keys[4], (D, D), D ** -0.5, 0.5)
    w_query = noise(keys[5], (D, D), D ** -0.5, 0.5)
    w_out = noise(keys[6], (D, D), D ** -0.5, 0.5)
    cotangent = noise(keys[7], (SENSORS, STEPS, D), 1.0, 6.0, ((0, 64), (1, 8)))
    return {"inputs": inputs, "mask": mask, "projector": projector, "w_key": w_key, "w_value": w_value, "w_query": w_query, "w_out": w_out, "cotangent": cotangent}


sharpness_divisor = 12.0
epsilon = 1e-06
largest_energy = lax.Precision.HIGHEST

def normalize(vector):
    return vector * lax.rsqrt(lax.optimization_barrier(jnp.mean(vector * vector, axis=-1, keepdims=True)) + epsilon)

def attend_in(matched_plain_vector, values, projector):
    matched_unit_vector = normalize(matched_plain_vector)
    mapping_unit_vector = normalize(projector)
    attention_energies = sharpness_divisor / matched_plain_vector.shape[-1] * jnp.dot(mapping_unit_vector, matched_unit_vector.T, precision=largest_energy)
    weights = jnp.exp(attention_energies)
    numerator = jnp.dot(weights, values.astype(jnp.float32), precision=largest_energy)
    denominator = lax.optimization_barrier(jnp.sum(weights, axis=1))
    return (numerator, denominator)

def make_summary(numerator, denominator):
    return numerator / denominator[..., None]

def attend_out(asking_plain_vector, summary):
    asking_unit_vector = normalize(asking_plain_vector)
    pooled_unit_vector = normalize(summary)
    attention_energies = sharpness_divisor / asking_plain_vector.shape[-1] * jnp.dot(asking_unit_vector, pooled_unit_vector.T, precision=largest_energy)
    weights = jnp.exp(attention_energies)
    weights = weights / lax.optimization_barrier(jnp.sum(weights, axis=1, keepdims=True))
    blended = jnp.dot(weights, summary, precision=largest_energy)
    return normalize(blended).astype(jnp.bfloat16)

def contract_rows(left, right):
    return lax.dot_general(left, right, (((0,), (0,)), ((), ())), preferred_element_type=jnp.float32)

def reference(inputs, mask, projector, w_key, w_value, w_query, w_out, cotangent):

    def one_step(totals, slices):
        rows, marks, incoming = slices
        hidden = rows * marks[:, None].astype(rows.dtype)
        matched_plain_vector = jnp.dot(hidden, w_key, preferred_element_type=jnp.float32)
        values = jnp.dot(hidden, w_value, preferred_element_type=jnp.float32).astype(jnp.bfloat16)
        asking_plain_vector = jnp.dot(hidden, w_query, preferred_element_type=jnp.float32)
        (numerator, denominator), in_back = jax.vjp(attend_in, matched_plain_vector, values, projector)
        summary, summary_back = jax.vjp(make_summary, numerator, denominator)
        normed, out_back = jax.vjp(attend_out, asking_plain_vector, summary)
        output_rows = (hidden.astype(jnp.float32) + jnp.dot(normed, w_out, preferred_element_type=jnp.float32)).astype(jnp.bfloat16)
        grad_out = contract_rows(normed, incoming)
        d_normed = jnp.dot(incoming, w_out.T, preferred_element_type=jnp.float32).astype(jnp.bfloat16)
        d_query, d_summary = out_back(d_normed)
        d_numerator, d_denominator = summary_back(d_summary)
        d_key, d_values, d_projector = in_back((d_numerator, d_denominator))
        d_query = d_query.astype(jnp.bfloat16)
        d_key = d_key.astype(jnp.bfloat16)
        grad_key = contract_rows(hidden, d_key)
        grad_value = contract_rows(hidden, d_values)
        grad_query = contract_rows(hidden, d_query)
        d_hidden = incoming.astype(jnp.float32)
        d_hidden = d_hidden + jnp.dot(d_query, w_query.T, preferred_element_type=jnp.float32)
        d_hidden = d_hidden + jnp.dot(d_key, w_key.T, preferred_element_type=jnp.float32)
        d_hidden = d_hidden + jnp.dot(d_values, w_value.T, preferred_element_type=jnp.float32)
        d_inputs = (d_hidden * marks[:, None].astype(jnp.float32)).astype(jnp.bfloat16)
        totals = (totals[0] + d_projector, totals[1] + grad_key, totals[2] + grad_value, totals[3] + grad_query, totals[4] + grad_out)
        return (totals, (output_rows, d_inputs))
    square = jnp.zeros((D, D), jnp.float32)
    start = (jnp.zeros((K, D), jnp.float32), square, square, square, square)
    totals, (outputs, d_inputs) = lax.scan(one_step, start, (jnp.swapaxes(inputs, 0, 1), jnp.swapaxes(mask, 0, 1), jnp.swapaxes(cotangent, 0, 1)))
    return (jnp.swapaxes(outputs, 0, 1), jnp.swapaxes(d_inputs, 0, 1), totals[0], totals[1], totals[2], totals[3], totals[4])
```

```python
import functools

import jax
import jax.numpy as jnp
from jax import lax
from jax.experimental import pallas as pl
from jax.experimental.pallas import tpu as pltpu
from jax.sharding import Mesh
from jax.sharding import PartitionSpec as P

AXES = ("sx", "sz", "ty", "tc")
SENSOR = ("sx", "sz")
TIME = ("ty", "tc")
MESH_ID = pl.DeviceIdType.MESH
SHARPNESS = 12.0
EPS = 1e-06
GROUP = 4
BF = jnp.bfloat16
F32 = jnp.float32


def mm(a, b):
    return lax.dot_general(a, b, (((1,), (0,)), ((), ())), preferred_element_type=F32)


def mm_nt(a, b):
    return lax.dot_general(a, b, (((1,), (1,)), ((), ())), preferred_element_type=F32)


def mm_tn(a, b):
    return lax.dot_general(a, b, (((0,), (0,)), ((), ())), preferred_element_type=F32)


def row_scale(v):
    return lax.rsqrt(jnp.mean(v * v, axis=-1, keepdims=True) + EPS)


def row_mean(v):
    return jnp.mean(v, axis=-1, keepdims=True)


def kernel(
    dims,
    x_ref, mask_ref, proj_ref, wk_ref, wv_ref, wq_ref, wo_ref, cot_ref,
    lo_ref, gi_ref, gp_ref, gk_ref, gv_ref, gq_ref, go_ref,
    rows, hid, kraw, vals, qraw, cott, dnorm, wexp, pre,
    num1, xb1, zs1, zb1, gs,
    num2, xb2, zs2, zb2, gd,
    dn, db, dz, dzb, dg,
    acc_p, acc_kv, acc_q, acc_o,
    grad, gt, xs, xr, zr, fa,
    xs_r, zs_r, ag_r, xag_r, misc_r, send,
):
    NX, NZ, NY, NC, n, T, K, D = dims
    KC = K // NX
    R = NY * NC
    RG, RP = D // R, K // R
    RX = 4 * RG // NX
    c = SHARPNESS / D
    x, z, y, core = [lax.axis_index(a) for a in AXES]
    r = y * NC + core

    def dev(ax, az, ay, ac):
        return (ax, az, ay, ac)

    xpeers = [lax.rem(x + d, NX) for d in range(1, NX)]
    zpeers = [lax.rem(z + d, NZ) for d in range(1, NZ)]
    rpeers = [lax.rem(r + d, R) for d in range(1, R)]

    barrier = pltpu.get_barrier_semaphore()
    for p in xpeers:
        pl.semaphore_signal(barrier, inc=1, device_id=dev(p, z, y, core), device_id_type=MESH_ID)
    for p in zpeers:
        pl.semaphore_signal(barrier, inc=1, device_id=dev(x, p, y, core), device_id_type=MESH_ID)
    for p in rpeers:
        pl.semaphore_signal(
            barrier, inc=1, device_id=dev(x, z, lax.div(p, NC), lax.rem(p, NC)), device_id_type=MESH_ID
        )

    def start(src, dst, s_sem, r_sem, device):
        pltpu.make_async_remote_copy(
            src_ref=src, dst_ref=dst, send_sem=s_sem, recv_sem=r_sem, device_id=device, device_id_type=MESH_ID
        ).start()

    def wait(ref, sem):
        pltpu.make_async_copy(ref, ref, sem).wait()

    def far_step(chunk, j):
        half = T // 2
        s = GROUP * chunk + j
        off = half + lax.div(s, 2) if j % 2 == 0 else half - lax.div(s + 1, 2)
        return lax.rem(z + off, T)

    def near_step(chunk, j):
        half = T // 2
        s = T - 1 - (GROUP * chunk + j)
        off = half + lax.div(s, 2) if j % 2 == 1 else half - lax.div(s + 1, 2)
        return lax.rem(z + off, T)

    chunks = T // GROUP
    lane_t = lax.broadcasted_iota(jnp.int32, (n, T), 1)

    def mask_column(t):
        return jnp.sum(jnp.where(lane_t == t, mask_ref[...].astype(F32), 0.0), axis=1, keepdims=True)

    proj = proj_ref[...]
    punit = proj * row_scale(proj)
    pu_b = punit.astype(BF)

    rows[...] = x_ref[...].reshape(n * T, D).astype(F32)
    dn[...] = jnp.zeros_like(dn)

    def send_columns(t, num, xb, phase):
        for d in range(1, NX):
            start(num.at[t, xpeers[d - 1]], xb.at[t, d - 1], send.at[2 * phase], xs_r.at[phase, t],
                  dev(xpeers[d - 1], z, y, core))

    def to_owner(t, num, xb, zs, zb, phase):
        wait(xb.at[t], xs_r.at[phase, t])
        total = num[t, x]
        for d in range(1, NX):
            total = total + xb[t, d - 1]
        zs[t] = total
        off = lax.rem(t - z + NZ, NZ)

        @pl.when(off == 0)
        def _():
            zb[0] = total

        @pl.when(off != 0)
        def _():
            start(zs.at[t], zb.at[off], send.at[2 * phase + 1], zs_r.at[phase], dev(x, t, y, core))

    def to_peers(t, g, phase):
        for d in range(1, NX):
            start(g.at[t, x], g.at[t, x], send.at[4 + 2 * phase], xag_r.at[phase, t],
                  dev(xpeers[d - 1], z, y, core))

    def gather_step(t, g, phase):
        @pl.when(t != z)
        def _():
            wait(g.at[t, x], ag_r.at[phase, t])

        to_peers(t, g, phase)

    def first(chunk):
        ts = [far_step(chunk, j) for j in range(GROUP)]
        hs = []
        for t in ts:
            h = (rows[pl.ds(t, n, stride=T), :] * mask_column(t)).astype(BF)
            hid[t] = h
            hs.append(h)
        h = jnp.concatenate(hs, axis=0)
        kr = mm(h, wk_ref[...])
        v = mm(h, wv_ref[...]).astype(BF)
        qr = mm(h, wq_ref[...])
        ku = kr * row_scale(kr)
        w = jnp.exp(c * mm_nt(ku.astype(BF), pu_b))
        wb = w.astype(BF)
        for j, t in enumerate(ts):
            own = slice(j * n, (j + 1) * n)
            kraw[t] = kr[own]
            vals[t] = v[own]
            qraw[t] = qr[own]
            wexp[t] = w[own]
            num1[t] = mm_tn(wb[own], v[own]).reshape(NX, KC, D)
            dn[t, :, 0:K] = jnp.sum(w[own], axis=0, keepdims=True)
        return ts

    def first_loop(chunk, _):
        ts = first(chunk)

        @pl.when(chunk == 0)
        def _():
            pl.semaphore_wait(barrier, NX - 1 + NZ - 1 + R - 1)

        for t in ts:
            send_columns(t, num1, xb1, 0)

        @pl.when(chunk >= 2)
        def _():
            for j in range(GROUP):
                to_owner(far_step(chunk - 2, j), num1, xb1, zs1, zb1, 0)

        return 0

    lax.fori_loop(0, chunks, first_loop, 0)
    for d in range(1, NX):
        start(dn, db.at[d - 1], send.at[8], misc_r.at[0], dev(xpeers[d - 1], z, y, core))
    if chunks >= 2:
        for j in range(GROUP):
            to_owner(far_step(chunks - 2, j), num1, xb1, zs1, zb1, 0)
    wait(db, misc_r.at[0])
    den = dn[...]
    for d in range(1, NX):
        den = den + db[d - 1]
    dz[...] = den
    for d in range(1, NZ):
        start(dz.at[zpeers[d - 1]], dzb.at[d], send.at[9], misc_r.at[1], dev(x, zpeers[d - 1], y, core))
    dzb[0] = dz[z]
    for j in range(GROUP):
        to_owner(far_step(chunks - 1, j), num1, xb1, zs1, zb1, 0)

    rows[...] = cot_ref[...].reshape(n * T, D).astype(F32)

    def cot_loop(chunk, _):
        ts = [chunk * GROUP + j for j in range(GROUP)]
        cs = []
        for t in ts:
            ct = rows[pl.ds(t, n, stride=T), :].astype(BF)
            cott[t] = ct
            cs.append(ct)
        d = mm_nt(jnp.concatenate(cs, axis=0), wo_ref[...]).astype(BF)
        for j, t in enumerate(ts):
            dnorm[t] = d[j * n:(j + 1) * n]
        return 0

    lax.fori_loop(0, chunks, cot_loop, 0)

    wait(dzb.at[pl.ds(1, NZ - 1)], misc_r.at[1])
    wait(zb1.at[pl.ds(1, NZ - 1)], zs_r.at[0])
    den_row = jnp.sum(dzb[...], axis=0)
    dg[z] = den_row
    numer = jnp.sum(zb1[...], axis=0)
    at = lax.broadcasted_iota(jnp.int32, (KC, D), 1) == lax.broadcasted_iota(jnp.int32, (KC, D), 0) + x * KC
    den_col = jnp.sum(jnp.where(at, den_row, 0.0), axis=1, keepdims=True)
    gs[z, x] = numer / den_col
    for d in range(1, NZ):
        start(gs.at[z, x], gs.at[z, x], send.at[5], ag_r.at[0, z], dev(x, zpeers[d - 1], y, core))
    for d in range(1, NZ):
        start(dg.at[z], dg.at[z], send.at[10], misc_r.at[2], dev(x, zpeers[d - 1], y, core))

    acc_q[...] = jnp.zeros_like(acc_q)
    acc_o[...] = jnp.zeros_like(acc_o)
    acc_kv[...] = jnp.zeros_like(acc_kv)
    acc_p[...] = jnp.zeros_like(acc_p)

    def second(chunk):
        ts = [near_step(chunk, j) for j in range(GROUP)]
        normeds, dqs = [], []
        for t in ts:
            wait(gs.at[t, pl.ds(0, NX - 1)], xag_r.at[0, t])
        for t in ts:
            s = gs[t].reshape(K, D)
            rs = row_scale(s)
            su = s * rs
            s_b = s.astype(BF)
            su_b = su.astype(BF)
            qr = qraw[t]
            rq = row_scale(qr)
            qu = qr * rq
            qu_b = qu.astype(BF)
            e = jnp.exp(c * mm_nt(qu_b, su_b))
            a = e / jnp.sum(e, axis=1, keepdims=True)
            a_b = a.astype(BF)
            blended = mm(a_b, s_b)
            rb = row_scale(blended)
            bn = blended * rb
            normeds.append(bn.astype(BF))
            dy = dnorm[t].astype(F32)
            dbl = rb * (dy - bn * row_mean(dy * bn))
            dbl_b = dbl.astype(BF)
            da = mm_nt(dbl_b, s_b)
            ds = a * (da - jnp.sum(a * da, axis=1, keepdims=True))
            ds_b = (c * ds).astype(BF)
            dqu = mm(ds_b, su_b)
            dsu = mm_tn(ds_b, qu_b)
            dqs.append((rq * (dqu - qu * row_mean(dqu * qu))).astype(BF))
            dsum = mm_tn(a_b, dbl_b) + rs * (dsu - su * row_mean(dsu * su))
            num2[t] = dsum.reshape(NX, KC, D)
        return ts, normeds, dqs

    def second_loop(chunk, _):
        @pl.when(chunk + 1 < chunks)
        def _():
            for j in range(GROUP):
                gather_step(near_step(chunk + 1, j), gs, 0)

        ts, normeds, dqs = second(chunk)
        for t in ts:
            send_columns(t, num2, xb2, 1)
        normed = jnp.concatenate(normeds, axis=0)
        dq = jnp.concatenate(dqs, axis=0)
        h = jnp.concatenate([hid[t] for t in ts], axis=0)
        ct = jnp.concatenate([cott[t] for t in ts], axis=0)
        lo = (h.astype(F32) + mm(normed, wo_ref[...])).astype(BF)
        part = ct.astype(F32) + mm_nt(dq, wq_ref[...])
        acc_o[...] += mm_tn(normed, ct)
        acc_q[...] += mm_tn(h, dq)
        for j, t in enumerate(ts):
            own = slice(j * n, (j + 1) * n)
            lo_ref[t] = lo[own]
            pre[t] = part[own]

        @pl.when(chunk >= 1)
        def _():
            for j in range(GROUP):
                to_owner(near_step(chunk - 1, j), num2, xb2, zs2, zb2, 1)

        return 0

    for j in range(GROUP):
        gather_step(near_step(0, j), gs, 0)
    lax.fori_loop(0, chunks, second_loop, 0)
    for j in range(GROUP):
        to_owner(near_step(chunks - 1, j), num2, xb2, zs2, zb2, 1)

    wait(dg.at[pl.ds(0, NZ - 1)], misc_r.at[2])
    wait(zb2.at[pl.ds(1, NZ - 1)], zs_r.at[1])
    gd[z, x] = jnp.sum(zb2[...], axis=0)
    for d in range(1, NZ):
        start(gd.at[z, x], gd.at[z, x], send.at[7], ag_r.at[1, z], dev(x, zpeers[d - 1], y, core))

    def third_loop(chunk, _):
        @pl.when(chunk + 1 < chunks)
        def _():
            for j in range(GROUP):
                gather_step(near_step(chunk + 1, j), gd, 1)

        ts = [near_step(chunk, j) for j in range(GROUP)]
        for t in ts:
            wait(gd.at[t, pl.ds(0, NX - 1)], xag_r.at[1, t])
        dsins, dvs = [], []
        for t in ts:
            dsum = gd[t].reshape(K, D)
            s = gs[t].reshape(K, D)
            d_b = dsum.astype(BF)
            wp = wexp[t] / dg[t][:, 0:K]
            prod = dsum * s
            prod_hi = prod.astype(BF)
            prod_lo = (prod - prod_hi.astype(F32)).astype(BF)
            ones = jnp.ones((8, D), BF)
            s_row = (mm_nt(ones, prod_hi) + mm_nt(ones, prod_lo))[0:1]
            dsin = wp * (mm_nt(vals[t], d_b) - s_row)
            dsins.append((c * dsin).astype(BF))
            dvs.append(mm(wp.astype(BF), d_b).astype(BF))
        ds_b = jnp.concatenate(dsins, axis=0)
        dv = jnp.concatenate(dvs, axis=0)
        kr = jnp.concatenate([kraw[t] for t in ts], axis=0)
        h = jnp.concatenate([hid[t] for t in ts], axis=0)
        rk = row_scale(kr)
        ku = kr * rk
        dku = mm(ds_b, pu_b)
        dk = (rk * (dku - ku * row_mean(dku * ku))).astype(BF)
        acc_p[...] += mm_tn(ds_b, ku.astype(BF))
        acc_kv[...] += mm_tn(h, jnp.concatenate([dk, dv], axis=1))
        dh = mm_nt(dk, wk_ref[...]) + mm_nt(dv, wv_ref[...])
        for j, t in enumerate(ts):
            gi_ref[t] = ((pre[t] + dh[j * n:(j + 1) * n]) * mask_column(t)).astype(BF)
        return 0

    for j in range(GROUP):
        gather_step(near_step(0, j), gd, 1)
    lax.fori_loop(0, chunks, third_loop, 0)

    grad[:, 0:RG, :] = acc_kv[:, 0:D].reshape(R, RG, D)
    grad[:, RG:2 * RG, :] = acc_kv[:, D:2 * D].reshape(R, RG, D)
    grad[:, 2 * RG:3 * RG, :] = acc_q[...].reshape(R, RG, D)
    grad[:, 3 * RG:4 * RG, :] = acc_o[...].reshape(R, RG, D)
    grad[:, 4 * RG:4 * RG + RP, :] = acc_p[...].reshape(R, RP, D)
    for d in range(1, R):
        p = rpeers[d - 1]
        start(grad.at[p], gt.at[d - 1], send.at[11], misc_r.at[3], dev(x, z, lax.div(p, NC), lax.rem(p, NC)))
    wait(gt, misc_r.at[3])
    total = grad[r]
    for d in range(1, R):
        total = total + gt[d - 1]
    for i in range(NX):
        xs[i, 0:RX, :] = total[i * RX:(i + 1) * RX]
        xs[i, RX:RX + RP, :] = total[4 * RG:4 * RG + RP]
    for d in range(1, NX):
        start(xs.at[xpeers[d - 1]], xr.at[x], send.at[12], misc_r.at[4], dev(xpeers[d - 1], z, y, core))
    xr[x] = xs[x]
    wait(xr.at[pl.ds(0, NX - 1)], misc_r.at[4])
    zr[z] = jnp.sum(xr[...], axis=0)
    for d in range(1, NZ):
        start(zr.at[z], zr.at[z], send.at[13], misc_r.at[5], dev(x, zpeers[d - 1], y, core))
    wait(zr.at[pl.ds(0, NZ - 1)], misc_r.at[5])
    done = jnp.sum(zr[...], axis=0)
    fa[x] = done[0:RX]
    for d in range(1, NX):
        start(fa.at[x], fa.at[x], send.at[14], misc_r.at[6], dev(xpeers[d - 1], z, y, core))
    dpu = done[RX:RX + RP]
    prow = proj_ref[pl.ds(pl.multiple_of(r * RP, RP), RP), :]
    rp = row_scale(prow)
    pun = prow * rp
    gp_ref[...] = rp * (dpu - pun * row_mean(dpu * pun))
    wait(fa.at[pl.ds(0, NX - 1)], misc_r.at[6])
    final = fa[...].reshape(4 * RG, D)
    gk_ref[...] = final[0:RG]
    gv_ref[...] = final[RG:2 * RG]
    gq_ref[...] = final[2 * RG:3 * RG]
    go_ref[...] = final[3 * RG:4 * RG]

    wait(xb1, send.at[0])
    wait(zb1.at[pl.ds(1, NZ - 1)], send.at[1])
    wait(xb2, send.at[2])
    wait(zb2.at[pl.ds(1, NZ - 1)], send.at[3])
    wait(gs.at[:, pl.ds(0, NX - 1)], send.at[4])
    wait(zb1.at[pl.ds(1, NZ - 1)], send.at[5])
    wait(gd.at[:, pl.ds(0, NX - 1)], send.at[6])
    wait(zb2.at[pl.ds(1, NZ - 1)], send.at[7])
    wait(db, send.at[8])
    wait(dzb.at[pl.ds(1, NZ - 1)], send.at[9])
    wait(dzb.at[pl.ds(1, NZ - 1)], send.at[10])
    wait(gt, send.at[11])
    wait(xr.at[pl.ds(0, NX - 1)], send.at[12])
    wait(zr.at[pl.ds(0, NZ - 1)], send.at[13])
    wait(fa.at[pl.ds(0, NX - 1)], send.at[14])


def per_device(dims, inputs, mask, projector, w_key, w_value, w_query, w_out, cotangent):
    NX, NZ, NY, NC, n, T, K, D = dims
    KC, R = K // NX, NY * NC
    RG, RP = D // R, K // R
    RX = 4 * RG // NX
    vm = pl.BlockSpec(memory_space=pltpu.VMEM)
    steps = jax.ShapeDtypeStruct((T, n, D), BF)
    part = jax.ShapeDtypeStruct((RG, D), F32)
    lo, gi, gp, gk, gv, gq, go = pl.pallas_call(
        functools.partial(kernel, dims),
        out_shape=(steps, steps, jax.ShapeDtypeStruct((RP, D), F32), part, part, part, part),
        in_specs=[vm] * 8,
        out_specs=(vm,) * 7,
        scratch_shapes=[
            pltpu.VMEM((n * T, D), F32),
            pltpu.VMEM((T, n, D), BF),
            pltpu.VMEM((T, n, D), F32),
            pltpu.VMEM((T, n, D), BF),
            pltpu.VMEM((T, n, D), F32),
            pltpu.VMEM((T, n, D), BF),
            pltpu.VMEM((T, n, D), BF),
            pltpu.VMEM((T, n, K), F32),
            pltpu.VMEM((T, n, D), F32),
            pltpu.VMEM((T, NX, KC, D), F32),
            pltpu.VMEM((T, NX - 1, KC, D), F32),
            pltpu.VMEM((T, KC, D), F32),
            pltpu.VMEM((NZ, KC, D), F32),
            pltpu.VMEM((T, NX, KC, D), F32),
            pltpu.VMEM((T, NX, KC, D), F32),
            pltpu.VMEM((T, NX - 1, KC, D), F32),
            pltpu.VMEM((T, KC, D), F32),
            pltpu.VMEM((NZ, KC, D), F32),
            pltpu.VMEM((T, NX, KC, D), F32),
            pltpu.VMEM((T, 1, D), F32),
            pltpu.VMEM((NX - 1, T, 1, D), F32),
            pltpu.VMEM((T, 1, D), F32),
            pltpu.VMEM((NZ, 1, D), F32),
            pltpu.VMEM((T, 1, D), F32),
            pltpu.VMEM((K, D), F32),
            pltpu.VMEM((D, 2 * D), F32),
            pltpu.VMEM((D, D), F32),
            pltpu.VMEM((D, D), F32),
            pltpu.VMEM((R, 4 * RG + RP, D), F32),
            pltpu.VMEM((R - 1, 4 * RG + RP, D), F32),
            pltpu.VMEM((NX, RX + RP, D), F32),
            pltpu.VMEM((NX, RX + RP, D), F32),
            pltpu.VMEM((NZ, RX + RP, D), F32),
            pltpu.VMEM((NX, RX, D), F32),
            pltpu.SemaphoreType.DMA((2, T)),
            pltpu.SemaphoreType.DMA((2,)),
            pltpu.SemaphoreType.DMA((2, T)),
            pltpu.SemaphoreType.DMA((2, T)),
            pltpu.SemaphoreType.DMA((7,)),
            pltpu.SemaphoreType.DMA((15,)),
        ],
        compiler_params=pltpu.CompilerParams(
            collective_id=0, has_side_effects=True, vmem_limit_bytes=48 << 20
        ),
    )(inputs, mask, projector, w_key, w_value, w_query, w_out, cotangent)
    return (jnp.swapaxes(lo, 0, 1), jnp.swapaxes(gi, 0, 1), gp, gk, gv, gq, go)


def build(torus, n, T, K, D):
    dims = tuple(torus.shape[a] for a in AXES) + (n, T, K, D)
    in_specs = (P(SENSOR, TIME, None), P(SENSOR, TIME), P(), P(), P(), P(), P(), P(SENSOR, TIME, None))
    rows = P(TIME, None)
    out_specs = (P(SENSOR, TIME, None), P(SENSOR, TIME, None), rows, rows, rows, rows, rows)
    return jax.shard_map(
        functools.partial(per_device, dims), mesh=torus, in_specs=in_specs, out_specs=out_specs, check_vma=False
    )


def solution(mesh):
    torus = Mesh(mesh.devices.reshape(4, 16, 4, 2), AXES)
    return build(torus, 4096 // 64, 128 // 8, 64, 128)
```

```python
import functools

import jax
import jax.numpy as jnp
from jax import lax
from jax.experimental import pallas as pl
from jax.experimental.pallas import tpu as pltpu
from jax.sharding import Mesh
from jax.sharding import PartitionSpec as P

AXES = ("sx", "sz", "ty", "tc")
SENSOR = ("sx", "sz")
TIME = ("ty", "tc")
MESH_ID = pl.DeviceIdType.MESH
SHARPNESS = 12.0
EPS = 1e-06
GROUP = 8
BF = jnp.bfloat16
F32 = jnp.float32


def mm(a, b):
    return lax.dot_general(a, b, (((1,), (0,)), ((), ())), preferred_element_type=F32)


def mm_nt(a, b):
    return lax.dot_general(a, b, (((1,), (1,)), ((), ())), preferred_element_type=F32)


def mm_tn(a, b):
    return lax.dot_general(a, b, (((0,), (0,)), ((), ())), preferred_element_type=F32)


def row_scale(v):
    return lax.rsqrt(jnp.mean(v * v, axis=-1, keepdims=True) + EPS)


def row_mean(v):
    return jnp.mean(v, axis=-1, keepdims=True)


def kernel(
    dims,
    x_hbm, mask_hbm, proj_hbm, wk_hbm, wv_hbm, wq_hbm, wo_hbm, cot_hbm,
    lo_ref, gi_ref, gp_ref, gk_ref, gv_ref, gq_ref, go_ref,
    x_ref, mask_ref, proj_ref, wk_ref, wv_ref, wq_ref, wo_ref, cot_ref,
    rows, hid, kraw, vals, qraw, cott, dnorm, wexp, pre,
    num1, xb1, zs1, zb1, gs,
    num2, xb2, zs2, zb2, gd,
    dn, db, dz, dzb, dg,
    acc_p, acc_kv, acc_q, acc_o,
    g_e, t_e, z_e, f_e, g_l, t_l, z_l, f_l, g_p, t_p, z_p, f_p,
    in_s, xs_r, zs_r, ag_r, xag_r, den_r, den_z, den_g, w_r, send, w_send,
):
    NX, NZ, NY, NC, n, T, K, D = dims
    KC = K // NX
    R = NY * NC
    RG, RP = D // R, K // R
    RX = 2 * RG // NX
    c = SHARPNESS / D
    x, z, y, core = [lax.axis_index(a) for a in AXES]
    r = y * NC + core

    def dev(ax, az, ay, ac):
        return (ax, az, ay, ac)

    def dev_r(ax, p):
        return (ax, z, lax.div(p, NC), lax.rem(p, NC))

    xpeers = [lax.rem(x + d, NX) for d in range(1, NX)]
    zpeers = [lax.rem(z + d, NZ) for d in range(1, NZ)]
    plane = [(dr, dx) for dr in range(R) for dx in range(NX) if dr or dx]

    barrier = pltpu.get_barrier_semaphore()
    for p in zpeers:
        pl.semaphore_signal(barrier, inc=1, device_id=dev(x, p, y, core), device_id_type=MESH_ID)
    for dr, dx in plane:
        pl.semaphore_signal(
            barrier, inc=1, device_id=dev_r(lax.rem(x + dx, NX), lax.rem(r + dr, R)), device_id_type=MESH_ID
        )

    loads = [
        pltpu.make_async_copy(a, b, in_s.at[i])
        for i, (a, b) in enumerate([
            (x_hbm, x_ref), (mask_hbm, mask_ref), (proj_hbm, proj_ref), (wk_hbm, wk_ref), (wv_hbm, wv_ref),
            (wq_hbm, wq_ref), (wo_hbm, wo_ref), (cot_hbm, cot_ref),
        ])
    ]
    for load in loads:
        load.start()

    def start(src, dst, s_sem, r_sem, device):
        pltpu.make_async_remote_copy(
            src_ref=src, dst_ref=dst, send_sem=s_sem, recv_sem=r_sem, device_id=device, device_id_type=MESH_ID
        ).start()

    def wait(ref, sem):
        pltpu.make_async_copy(ref, ref, sem).wait()

    def far_step(chunk, j):
        half = T // 2
        s = GROUP * chunk + j
        off = half + lax.div(s, 2) if j % 2 == 0 else half - lax.div(s + 1, 2)
        return lax.rem(z + off, T)

    def near_step(chunk, j):
        half = T // 2
        s = T - 1 - (GROUP * chunk + j)
        off = half + lax.div(s, 2) if j % 2 == 1 else half - lax.div(s + 1, 2)
        return lax.rem(z + off, T)

    chunks = T // GROUP
    diagonal = lax.broadcasted_iota(jnp.int32, (n, n), 0) == lax.broadcasted_iota(jnp.int32, (n, n), 1)

    def mask_column(t):
        row = mask_ref[pl.ds(t, 1), :].astype(F32)
        return jnp.sum(jnp.where(diagonal, row, 0.0), axis=1, keepdims=True)

    dn[...] = jnp.zeros_like(dn)
    for load in loads[:6]:
        load.wait()
    proj = proj_ref[...]
    punit = proj * row_scale(proj)
    pu_b = punit.astype(BF)

    rows[...] = x_ref[...].reshape(n * T, D).astype(F32)

    def send_columns(t, num, xb, phase):
        for d in range(1, NX):
            start(num.at[t, xpeers[d - 1]], xb.at[t, d - 1], send.at[2 * phase], xs_r.at[phase, t],
                  dev(xpeers[d - 1], z, y, core))

    def to_owner(t, num, xb, zs, zb, phase):
        wait(xb.at[t], xs_r.at[phase, t])
        total = num[t, x]
        for d in range(1, NX):
            total = total + xb[t, d - 1]
        zs[t] = total
        off = lax.rem(t - z + NZ, NZ)

        @pl.when(off == 0)
        def _():
            zb[0] = total

        @pl.when(off != 0)
        def _():
            start(zs.at[t], zb.at[off], send.at[2 * phase + 1], zs_r.at[phase], dev(x, t, y, core))

    def to_peers(t, g, phase):
        for d in range(1, NX):
            start(g.at[t, x], g.at[t, x], send.at[4 + 2 * phase], xag_r.at[phase, t],
                  dev(xpeers[d - 1], z, y, core))

    def gather_step(t, g, phase):
        @pl.when(t != z)
        def _():
            wait(g.at[t, x], ag_r.at[phase, t])

        to_peers(t, g, phase)

    def first(chunk):
        ts = [far_step(chunk, j) for j in range(GROUP)]
        hs = []
        for t in ts:
            h = (rows[pl.ds(t, n, stride=T), :] * mask_column(t)).astype(BF)
            hid[t] = h
            hs.append(h)
        h = jnp.concatenate(hs, axis=0)
        kr = mm(h, wk_ref[...])
        v = mm(h, wv_ref[...]).astype(BF)
        qr = mm(h, wq_ref[...])
        ku = kr * row_scale(kr)
        w = jnp.exp(c * mm_nt(ku.astype(BF), pu_b))
        wb = w.astype(BF)
        for j, t in enumerate(ts):
            own = slice(j * n, (j + 1) * n)
            kraw[t] = kr[own]
            vals[t] = v[own]
            qraw[t] = qr[own]
            wexp[t] = w[own]
            num1[t] = mm_tn(wb[own], v[own]).reshape(NX, KC, D)
            dn[chunk * GROUP + j, :, 0:K] = jnp.sum(w[own], axis=0, keepdims=True)
        return ts

    def first_loop(chunk, _):
        ts = first(chunk)

        @pl.when(chunk == 0)
        def _():
            pl.semaphore_wait(barrier, NZ - 1 + R * NX - 1)

        mine = pl.ds(chunk * GROUP, GROUP)
        for d in range(1, NX):
            start(dn.at[mine], db.at[d - 1, mine], send.at[8], den_r.at[chunk], dev(xpeers[d - 1], z, y, core))
        for t in ts:
            send_columns(t, num1, xb1, 0)
        return 0

    def den_to_owner(chunk):
        mine = pl.ds(chunk * GROUP, GROUP)
        wait(db.at[pl.ds(0, NX - 1), mine], den_r.at[chunk])
        total = dn[mine]
        for d in range(1, NX):
            total = total + db[d - 1, mine]
        dz[mine] = total
        for j in range(GROUP):
            t = far_step(chunk, j)
            off = lax.rem(t - z + NZ, NZ)
            if chunk == chunks - 1 and j == GROUP - 1:
                dzb[0] = total[j]
            else:
                start(dz.at[chunk * GROUP + j], dzb.at[off], send.at[9], den_z, dev(x, t, y, core))

    lax.fori_loop(0, chunks, first_loop, 0)
    for chunk in range(chunks):
        den_to_owner(chunk)
        for j in range(GROUP):
            to_owner(far_step(chunk, j), num1, xb1, zs1, zb1, 0)

    loads[6].wait()
    loads[7].wait()
    rows[...] = cot_ref[...].reshape(n * T, D).astype(F32)

    def cot_loop(chunk, _):
        ts = [chunk * GROUP + j for j in range(GROUP)]
        cs = []
        for t in ts:
            ct = rows[pl.ds(t, n, stride=T), :].astype(BF)
            cott[t] = ct
            cs.append(ct)
        d = mm_nt(jnp.concatenate(cs, axis=0), wo_ref[...]).astype(BF)
        for j, t in enumerate(ts):
            dnorm[t] = d[j * n:(j + 1) * n]
        return 0

    lax.fori_loop(0, chunks, cot_loop, 0)

    wait(dzb.at[pl.ds(1, NZ - 1)], den_z)
    wait(zb1.at[pl.ds(1, NZ - 1)], zs_r.at[0])
    den_row = jnp.sum(dzb[...], axis=0)
    dg[z] = den_row
    numer = jnp.sum(zb1[...], axis=0)
    at = lax.broadcasted_iota(jnp.int32, (KC, D), 1) == lax.broadcasted_iota(jnp.int32, (KC, D), 0) + x * KC
    den_col = jnp.sum(jnp.where(at, den_row, 0.0), axis=1, keepdims=True)
    gs[z, x] = numer / den_col
    for d in range(1, NZ):
        start(gs.at[z, x], gs.at[z, x], send.at[5], ag_r.at[0, z], dev(x, zpeers[d - 1], y, core))
    for d in range(1, NZ):
        start(dg.at[z], dg.at[z], send.at[10], den_g, dev(x, zpeers[d - 1], y, core))

    acc_q[...] = jnp.zeros_like(acc_q)
    acc_o[...] = jnp.zeros_like(acc_o)
    acc_kv[...] = jnp.zeros_like(acc_kv)
    acc_p[...] = jnp.zeros_like(acc_p)

    def second(chunk):
        ts = [near_step(chunk, j) for j in range(GROUP)]
        normeds, dqs = [], []
        for t in ts:
            wait(gs.at[t, pl.ds(0, NX - 1)], xag_r.at[0, t])
        for t in ts:
            s = gs[t].reshape(K, D)
            rs = row_scale(s)
            su = s * rs
            s_b = s.astype(BF)
            su_b = su.astype(BF)
            qr = qraw[t]
            rq = row_scale(qr)
            qu = qr * rq
            qu_b = qu.astype(BF)
            e = jnp.exp(c * mm_nt(qu_b, su_b))
            dy = dnorm[t].astype(F32)
            mixed = mm(e.astype(BF), s_b)
            inv = 1.0 / jnp.sum(e, axis=1, keepdims=True)
            rb = lax.rsqrt(row_mean(mixed * mixed) * (inv * inv) + EPS)
            scale = rb * inv
            bn = mixed * scale
            normeds.append(bn.astype(BF))
            dbl = rb * (dy - bn * (scale * row_mean(dy * mixed)))
            a = e * inv
            a_b = a.astype(BF)
            dbl_b = dbl.astype(BF)
            da = mm_nt(dbl_b, s_b)
            ds = a * (da - jnp.sum(a * da, axis=1, keepdims=True))
            ds_b = (c * ds).astype(BF)
            dqu = mm(ds_b, su_b)
            dsu = mm_tn(ds_b, qu_b)
            dqs.append((rq * (dqu - qu * row_mean(dqu * qu))).astype(BF))
            dsum = mm_tn(a_b, dbl_b) + rs * (dsu - su * row_mean(dsu * su))
            num2[t] = dsum.reshape(NX, KC, D)
        return ts, normeds, dqs

    def second_loop(chunk, _):
        @pl.when(chunk + 1 < chunks)
        def _():
            for j in range(GROUP):
                gather_step(near_step(chunk + 1, j), gs, 0)

        ts, normeds, dqs = second(chunk)
        for t in ts:
            send_columns(t, num2, xb2, 1)
        normed = jnp.concatenate(normeds, axis=0)
        dq = jnp.concatenate(dqs, axis=0)
        h = jnp.concatenate([hid[t] for t in ts], axis=0)
        ct = jnp.concatenate([cott[t] for t in ts], axis=0)
        lo = h.astype(F32) + mm(normed, wo_ref[...])
        part = ct.astype(F32) + mm_nt(dq, wq_ref[...])
        acc_o[...] += mm_tn(normed, ct)
        acc_q[...] += mm_tn(h, dq)
        for j, t in enumerate(ts):
            own = slice(j * n, (j + 1) * n)
            rows[pl.ds(t, n, stride=T), :] = lo[own]
            pre[t] = part[own]

        @pl.when(chunk >= 1)
        def _():
            for j in range(GROUP):
                to_owner(near_step(chunk - 1, j), num2, xb2, zs2, zb2, 1)

        return 0

    for j in range(GROUP):
        gather_step(near_step(0, j), gs, 0)
    lax.fori_loop(0, chunks, second_loop, 0)
    for j in range(GROUP):
        to_owner(near_step(chunks - 1, j), num2, xb2, zs2, zb2, 1)

    half = NX // 2
    g_e[:, 0:half] = acc_q[...].reshape(R, half, RX, D)
    g_e[:, half:NX] = acc_o[...].reshape(R, half, RX, D)

    def to_rows(g, t_buf, k):
        for dr, dx in plane:
            px, pr = lax.rem(x + dx, NX), lax.rem(r + dr, R)
            start(g.at[pr, px], t_buf.at[dr * NX + dx], w_send.at[k], w_r.at[k], dev_r(px, pr))
        t_buf[0] = g[r, x]

    def along_z(t_buf, z_buf, k):
        wait(t_buf.at[pl.ds(1, R * NX - 1)], w_r.at[k])
        z_buf[z] = jnp.sum(t_buf[...], axis=0)
        for d in range(1, NZ):
            start(z_buf.at[z], z_buf.at[z], w_send.at[k + 1], w_r.at[k + 1], dev(x, zpeers[d - 1], y, core))

    def along_x(z_buf, f_buf, k):
        wait(z_buf.at[pl.ds(0, NZ - 1)], w_r.at[k + 1])
        f_buf[x] = jnp.sum(z_buf[...], axis=0)
        for d in range(1, NX):
            start(f_buf.at[x], f_buf.at[x], w_send.at[k + 2], w_r.at[k + 2], dev(xpeers[d - 1], z, y, core))

    to_rows(g_e, t_e, 0)
    lo_ref[...] = rows[...].astype(BF).reshape(n, T, D)

    wait(dg.at[pl.ds(0, NZ - 1)], den_g)
    wait(zb2.at[pl.ds(1, NZ - 1)], zs_r.at[1])
    gd[z, x] = jnp.sum(zb2[...], axis=0)
    for d in range(1, NZ):
        start(gd.at[z, x], gd.at[z, x], send.at[7], ag_r.at[1, z], dev(x, zpeers[d - 1], y, core))
    along_z(t_e, z_e, 0)

    def third_loop(chunk, _):
        @pl.when(chunk + 1 < chunks)
        def _():
            for j in range(GROUP):
                gather_step(near_step(chunk + 1, j), gd, 1)

        ts = [near_step(chunk, j) for j in range(GROUP)]
        for t in ts:
            wait(gd.at[t, pl.ds(0, NX - 1)], xag_r.at[1, t])
        dsins, dvs = [], []
        for t in ts:
            dsum = gd[t].reshape(K, D)
            s = gs[t].reshape(K, D)
            d_b = dsum.astype(BF)
            wp = wexp[t] * (1.0 / dg[t][:, 0:K])
            prod = dsum * s
            prod_hi = prod.astype(BF)
            prod_lo = (prod - prod_hi.astype(F32)).astype(BF)
            ones = jnp.ones((8, D), BF)
            s_row = (mm_nt(ones, prod_hi) + mm_nt(ones, prod_lo))[0:1]
            dsin = wp * (mm_nt(vals[t], d_b) - s_row)
            dsins.append((c * dsin).astype(BF))
            dvs.append(mm(wp.astype(BF), d_b).astype(BF))
        ds_b = jnp.concatenate(dsins, axis=0)
        dv = jnp.concatenate(dvs, axis=0)
        kr = jnp.concatenate([kraw[t] for t in ts], axis=0)
        h = jnp.concatenate([hid[t] for t in ts], axis=0)
        rk = row_scale(kr)
        ku = kr * rk
        dku = mm(ds_b, pu_b)
        dk = (rk * (dku - ku * row_mean(dku * ku))).astype(BF)
        acc_p[...] += mm_tn(ds_b, ku.astype(BF))
        acc_kv[...] += mm_tn(h, jnp.concatenate([dk, dv], axis=1))
        dh = mm_nt(dk, wk_ref[...]) + mm_nt(dv, wv_ref[...])
        for j, t in enumerate(ts):
            rows[pl.ds(t, n, stride=T), :] = (pre[t] + dh[j * n:(j + 1) * n]) * mask_column(t)
        return 0

    for j in range(GROUP):
        gather_step(near_step(0, j), gd, 1)
    lax.fori_loop(0, chunks, third_loop, 0)

    g_l[:, 0:half] = acc_kv[:, 0:D].reshape(R, half, RX, D)
    g_l[:, half:NX] = acc_kv[:, D:2 * D].reshape(R, half, RX, D)
    g_p[...] = acc_p[...].reshape(R, RP, D)
    to_rows(g_l, t_l, 3)
    for dr in range(R):
        pr = lax.rem(r + dr, R)
        px = lax.rem(pr, NX)
        dx = lax.rem(px - x + NX, NX)
        if dr:
            start(g_p.at[pr], t_p.at[dr * NX + dx], w_send.at[6], w_r.at[6], dev_r(px, pr))
        else:
            @pl.when(dx == 0)
            def _():
                t_p[0] = g_p[r]

            @pl.when(dx != 0)
            def _():
                start(g_p.at[r], t_p.at[dx], w_send.at[9], w_r.at[6], dev_r(px, r))
    meets = x == lax.rem(r, NX)
    along_x(z_e, f_e, 0)
    gi_ref[...] = rows[...].astype(BF).reshape(n, T, D)
    along_z(t_l, z_l, 3)

    @pl.when(meets)
    def _():
        along_z(t_p, z_p, 6)

    along_x(z_l, f_l, 3)

    @pl.when(meets)
    def _():
        wait(z_p.at[pl.ds(0, NZ - 1)], w_r.at[7])
        dpu = jnp.sum(z_p[...], axis=0)
        prow = proj_ref[pl.ds(pl.multiple_of(r * RP, RP), RP), :]
        rp = row_scale(prow)
        pun = prow * rp
        f_p[...] = rp * (dpu - pun * row_mean(dpu * pun))
        for d in range(1, NX):
            start(f_p, f_p, w_send.at[8], w_r.at[8], dev(xpeers[d - 1], z, y, core))

    wait(f_e.at[pl.ds(0, NX - 1)], w_r.at[2])
    final = f_e[...].reshape(2 * RG, D)
    gq_ref[...] = final[0:RG]
    go_ref[...] = final[RG:2 * RG]
    wait(f_l.at[pl.ds(0, NX - 1)], w_r.at[5])
    final = f_l[...].reshape(2 * RG, D)
    gk_ref[...] = final[0:RG]
    gv_ref[...] = final[RG:2 * RG]

    @pl.when(jnp.logical_not(meets))
    def _():
        wait(f_p, w_r.at[8])

    gp_ref[...] = f_p[...]

    wait(xb1, send.at[0])
    wait(zb1.at[pl.ds(1, NZ - 1)], send.at[1])
    wait(xb2, send.at[2])
    wait(zb2.at[pl.ds(1, NZ - 1)], send.at[3])
    wait(gs.at[:, pl.ds(0, NX - 1)], send.at[4])
    wait(zb1.at[pl.ds(1, NZ - 1)], send.at[5])
    wait(gd.at[:, pl.ds(0, NX - 1)], send.at[6])
    wait(zb2.at[pl.ds(1, NZ - 1)], send.at[7])
    wait(db, send.at[8])
    wait(dzb.at[pl.ds(1, NZ - 1)], send.at[9])
    wait(dzb.at[pl.ds(1, NZ - 1)], send.at[10])
    for k, t_buf, z_buf, f_buf in ((0, t_e, z_e, f_e), (3, t_l, z_l, f_l)):
        wait(t_buf.at[pl.ds(1, R * NX - 1)], w_send.at[k])
        wait(z_buf.at[pl.ds(0, NZ - 1)], w_send.at[k + 1])
        wait(f_buf.at[pl.ds(0, NX - 1)], w_send.at[k + 2])
    wait(g_p.at[pl.ds(0, R - 1)], w_send.at[6])

    @pl.when(jnp.logical_not(meets))
    def _():
        wait(f_p, w_send.at[9])

    @pl.when(meets)
    def _():
        wait(z_p.at[pl.ds(0, NZ - 1)], w_send.at[7])
        wait(t_p.at[pl.ds(0, NX - 1)], w_send.at[8])


def hand_out(*refs):
    sem = refs[-1]
    copies = [pltpu.make_async_copy(refs[i], refs[i + 7], sem.at[i]) for i in range(7)]
    for copy in copies:
        copy.start()
    for copy in copies:
        copy.wait()


def per_device(dims, inputs, mask, projector, w_key, w_value, w_query, w_out, cotangent):
    NX, NZ, NY, NC, n, T, K, D = dims
    KC, R = K // NX, NY * NC
    RG, RP = D // R, K // R
    RX = 2 * RG // NX
    hbm = pl.BlockSpec(memory_space=pltpu.HBM)
    vm = pl.BlockSpec(memory_space=pltpu.VMEM)
    steps = jax.ShapeDtypeStruct((n, T, D), BF)
    part = jax.ShapeDtypeStruct((RG, D), F32)
    operands = [
        pltpu.with_memory_space_constraint(a, pltpu.HBM)
        for a in (inputs, jnp.swapaxes(mask, 0, 1), projector, w_key, w_value, w_query, w_out, cotangent)
    ]
    lo, gi, gp, gk, gv, gq, go = pl.pallas_call(
        functools.partial(kernel, dims),
        out_shape=(steps, steps, jax.ShapeDtypeStruct((RP, D), F32), part, part, part, part),
        in_specs=[hbm] * 8,
        out_specs=(vm,) * 7,
        scratch_shapes=[
            pltpu.VMEM((n, T, D), BF),
            pltpu.VMEM((T, n), jnp.int32),
            pltpu.VMEM((K, D), F32),
            pltpu.VMEM((D, D), BF),
            pltpu.VMEM((D, D), BF),
            pltpu.VMEM((D, D), BF),
            pltpu.VMEM((D, D), BF),
            pltpu.VMEM((n, T, D), BF),
            pltpu.VMEM((n * T, D), F32),
            pltpu.VMEM((T, n, D), BF),
            pltpu.VMEM((T, n, D), F32),
            pltpu.VMEM((T, n, D), BF),
            pltpu.VMEM((T, n, D), F32),
            pltpu.VMEM((T, n, D), BF),
            pltpu.VMEM((T, n, D), BF),
            pltpu.VMEM((T, n, K), F32),
            pltpu.VMEM((T, n, D), F32),
            pltpu.VMEM((T, NX, KC, D), F32),
            pltpu.VMEM((T, NX - 1, KC, D), F32),
            pltpu.VMEM((T, KC, D), F32),
            pltpu.VMEM((NZ, KC, D), F32),
            pltpu.VMEM((T, NX, KC, D), F32),
            pltpu.VMEM((T, NX, KC, D), F32),
            pltpu.VMEM((T, NX - 1, KC, D), F32),
            pltpu.VMEM((T, KC, D), F32),
            pltpu.VMEM((NZ, KC, D), F32),
            pltpu.VMEM((T, NX, KC, D), F32),
            pltpu.VMEM((T, 1, D), F32),
            pltpu.VMEM((NX - 1, T, 1, D), F32),
            pltpu.VMEM((T, 1, D), F32),
            pltpu.VMEM((NZ, 1, D), F32),
            pltpu.VMEM((T, 1, D), F32),
            pltpu.VMEM((K, D), F32),
            pltpu.VMEM((D, 2 * D), F32),
            pltpu.VMEM((D, D), F32),
            pltpu.VMEM((D, D), F32),
            pltpu.VMEM((R, NX, RX, D), F32),
            pltpu.VMEM((R * NX, RX, D), F32),
            pltpu.VMEM((NZ, RX, D), F32),
            pltpu.VMEM((NX, RX, D), F32),
            pltpu.VMEM((R, NX, RX, D), F32),
            pltpu.VMEM((R * NX, RX, D), F32),
            pltpu.VMEM((NZ, RX, D), F32),
            pltpu.VMEM((NX, RX, D), F32),
            pltpu.VMEM((R, RP, D), F32),
            pltpu.VMEM((R * NX, RP, D), F32),
            pltpu.VMEM((NZ, RP, D), F32),
            pltpu.VMEM((RP, D), F32),
            pltpu.SemaphoreType.DMA((8,)),
            pltpu.SemaphoreType.DMA((2, T)),
            pltpu.SemaphoreType.DMA((2,)),
            pltpu.SemaphoreType.DMA((2, T)),
            pltpu.SemaphoreType.DMA((2, T)),
            pltpu.SemaphoreType.DMA((T // GROUP,)),
            pltpu.SemaphoreType.DMA,
            pltpu.SemaphoreType.DMA,
            pltpu.SemaphoreType.DMA((9,)),
            pltpu.SemaphoreType.DMA((11,)),
            pltpu.SemaphoreType.DMA((10,)),
        ],
        compiler_params=pltpu.CompilerParams(
            collective_id=0, has_side_effects=True, vmem_limit_bytes=48 << 20
        ),
    )(*operands)
    return tuple(
        pl.pallas_call(
            hand_out,
            out_shape=tuple(jax.ShapeDtypeStruct(a.shape, a.dtype) for a in (lo, gi, gp, gk, gv, gq, go)),
            in_specs=[vm] * 7,
            out_specs=(hbm,) * 7,
            scratch_shapes=[pltpu.SemaphoreType.DMA((7,))],
            compiler_params=pltpu.CompilerParams(vmem_limit_bytes=4 << 20),
        )(lo, gi, gp, gk, gv, gq, go)
    )


def build(torus, n, T, K, D):
    dims = tuple(torus.shape[a] for a in AXES) + (n, T, K, D)
    in_specs = (P(SENSOR, TIME, None), P(SENSOR, TIME), P(), P(), P(), P(), P(), P(SENSOR, TIME, None))
    rows = P(TIME, None)
    out_specs = (P(SENSOR, TIME, None), P(SENSOR, TIME, None), rows, rows, rows, rows, rows)
    return jax.shard_map(
        functools.partial(per_device, dims), mesh=torus, in_specs=in_specs, out_specs=out_specs, check_vma=False
    )


def solution(mesh):
    torus = Mesh(mesh.devices.reshape(4, 16, 4, 2), AXES)
    return build(torus, 4096 // 64, 128 // 8, 64, 128)
```

```python
import functools

import jax
import jax.numpy as jnp
from jax import lax
from jax.experimental import pallas as pl
from jax.experimental.pallas import tpu as pltpu
from jax.sharding import Mesh
from jax.sharding import PartitionSpec as P

AXES = ("sx", "sz", "ty", "tc")
SENSOR = ("sx", "sz")
TIME = ("ty", "tc")
MESH_ID = pl.DeviceIdType.MESH
SHARPNESS = 12.0
EPS = 1e-06
GROUP = 8
SENT = 4
HALVES = 2
BF = jnp.bfloat16
F32 = jnp.float32


def mm(a, b):
    return lax.dot_general(a, b, (((1,), (0,)), ((), ())), preferred_element_type=F32)


def mm_nt(a, b):
    return lax.dot_general(a, b, (((1,), (1,)), ((), ())), preferred_element_type=F32)


def mm_tn(a, b):
    return lax.dot_general(a, b, (((0,), (0,)), ((), ())), preferred_element_type=F32)


def row_scale(v):
    return lax.rsqrt(jnp.mean(v * v, axis=-1, keepdims=True) + EPS)


def row_mean(v):
    return jnp.mean(v, axis=-1, keepdims=True)


def stack(parts):
    return jnp.concatenate(parts, axis=0)


def kernel(
    dims,
    x_hbm, mask_hbm, proj_hbm, wk_hbm, wv_hbm, wq_hbm, wo_hbm, cot_hbm,
    lo_ref, gi_ref, gp_ref, gk_ref, gv_ref, gq_ref, go_ref,
    x_ref, mask_ref, proj_ref, wk_ref, wv_ref, wq_ref, wo_ref, cot_ref,
    rows, hid, kunit, kscale, vals, qunit, qscale, cott, dnorm, wexp, pre,
    num1, xb1, zs1, zb1, gs,
    num2, xb2, zs2, zb2, gd,
    dn, db, dz, dzb, dg,
    acc_p, acc_kv, acc_q, acc_o,
    g_e, t_e, z_e, f_e, g_l, t_l, z_l, f_l, g_p, t_p, z_p, f_p,
    in_s, xs_r, zs_r, ag_r, xag_r, den_r, den_z, den_g, w_r, send, w_send,
):
    NX, NZ, NY, NC, n, T, K, D = dims
    KC = K // NX
    KH = KC // HALVES
    R = NY * NC
    RG, RP = D // R, K // R
    RX = 2 * RG // NX
    c = SHARPNESS / D
    x, z, y, core = [lax.axis_index(a) for a in AXES]
    r = y * NC + core

    def dev(ax, az, ay, ac):
        return (ax, az, ay, ac)

    def dev_r(ax, p):
        return (ax, z, lax.div(p, NC), lax.rem(p, NC))

    xpeers = [lax.rem(x + d, NX) for d in range(1, NX)]
    zpeers = [lax.rem(z + d, NZ) for d in range(1, NZ)]
    plane = [(dr, dx) for dr in range(R) for dx in range(NX) if dr or dx]

    loads = [
        pltpu.make_async_copy(a, b, in_s.at[i])
        for i, (a, b) in enumerate([
            (x_hbm, x_ref), (mask_hbm, mask_ref), (proj_hbm, proj_ref), (wk_hbm, wk_ref), (wv_hbm, wv_ref),
            (wq_hbm, wq_ref), (wo_hbm, wo_ref), (cot_hbm, cot_ref),
        ])
    ]
    for load in loads:
        load.start()

    barrier = pltpu.get_barrier_semaphore()
    for p in zpeers:
        pl.semaphore_signal(barrier, inc=1, device_id=dev(x, p, y, core), device_id_type=MESH_ID)
    for dr, dx in plane:
        pl.semaphore_signal(
            barrier, inc=1, device_id=dev_r(lax.rem(x + dx, NX), lax.rem(r + dr, R)), device_id_type=MESH_ID
        )

    def start(src, dst, s_sem, r_sem, device):
        pltpu.make_async_remote_copy(
            src_ref=src, dst_ref=dst, send_sem=s_sem, recv_sem=r_sem, device_id=device, device_id_type=MESH_ID
        ).start()

    def wait(ref, sem):
        pltpu.make_async_copy(ref, ref, sem).wait()

    def step_at(chunk, j):
        ahead = GROUP // 2 * chunk + (j + 1) // 2
        return lax.rem(z + (T - ahead if j % 2 else ahead), T)

    def position(off):
        return 2 * off if off < T - off else 2 * (T - off) - 1

    chunks = T // GROUP
    ones = jnp.ones((D, D), BF)
    diagonal = lax.broadcasted_iota(jnp.int32, (n, n), 0) == lax.broadcasted_iota(jnp.int32, (n, n), 1)

    def mask_of(t):
        return jnp.where(diagonal, mask_ref[pl.ds(t, 1), :].astype(F32), 0.0).astype(BF)

    def means(v):
        return mm(v.astype(BF), ones) * (1.0 / D)

    dn[...] = jnp.zeros_like(dn)
    for load in loads[:6]:
        load.wait()
    proj = proj_ref[...]
    punit = proj * row_scale(proj)
    pu_b = punit.astype(BF)

    rows[...] = x_ref[...].reshape(n * T, D).astype(F32)

    def send_columns(g, h, num, xb, phase):
        some = pl.ds(g * SENT, SENT)
        for d in range(1, NX):
            start(num.at[some, xpeers[d - 1], h], xb.at[some, h, d - 1], send.at[2 * phase], xs_r.at[phase, h, g],
                  dev(xpeers[d - 1], z, y, core))

    def to_owner(g, h, num, xb, zs, zb, phase):
        wait(xb.at[pl.ds(g * SENT, SENT), h], xs_r.at[phase, h, g])
        for k in range(SENT):
            at = g * SENT + k
            total = num[at, x, h]
            for d in range(1, NX):
                total = total + xb[at, h, d - 1]
            if at == 0:
                zb[h, 0] = total
            else:
                zs[at, h] = total
                off = T - (at + 1) // 2 if at % 2 else at // 2
                start(zs.at[at, h], zb.at[h, off], send.at[2 * phase + 1], zs_r.at[phase, h],
                      dev(x, zpeers[off - 1], y, core))

    def den_to_owner(chunk):
        mine = pl.ds(chunk * GROUP, GROUP)
        wait(db.at[pl.ds(0, NX - 1), mine], den_r.at[chunk])
        total = dn[mine]
        for d in range(1, NX):
            total = total + db[d - 1, mine]
        dz[mine] = total
        for j in range(GROUP):
            at = chunk * GROUP + j
            off = T - (at + 1) // 2 if at % 2 else at // 2
            if at == 0:
                dzb[0] = total[0]
            else:
                start(dz.at[at], dzb.at[off], send.at[9], den_z, dev(x, zpeers[off - 1], y, core))

    def to_z(g, h, phase):
        for d in sorted(range(1, NZ), key=lambda d: min(d, NZ - d)):
            at = position(NZ - d)
            start(g.at[0, x, h], g.at[at, x, h], send.at[5 + 2 * phase], ag_r.at[phase, h, at // SENT],
                  dev(x, zpeers[d - 1], y, core))

    def forward(k, h, g, phase):
        some = pl.ds(k * SENT, SENT)
        came = some if k else pl.ds(1, SENT - 1)
        wait(g.at[came, x, h], ag_r.at[phase, h, k])
        for d in range(1, NX):
            start(g.at[some, x, h], g.at[some, x, h], send.at[4 + 2 * phase], xag_r.at[phase, h, k],
                  dev(xpeers[d - 1], z, y, core))

    def gather(g, phase):
        units = sorted(((k, h) for k in range(T // SENT) for h in range(HALVES)), key=lambda u: (u[0] + 1.5 * u[1], u[1]))
        for k, h in units:
            forward(k, h, g, phase)

    def gathered(chunk, g, phase):
        for k in range(GROUP // SENT):
            p = chunk * (GROUP // SENT) + k
            for h in range(HALVES):
                wait(g.at[pl.ds(p * SENT, SENT), pl.ds(0, NX - 1), h], xag_r.at[phase, h, p])

    per_chunk = GROUP // SENT

    def first_loop(step, _):
        chunk = chunks - 1 - step
        ts = [step_at(chunk, j) for j in range(GROUP)]
        hs = []
        for j, t in enumerate(ts):
            hs.append(mm(mask_of(t), rows[pl.ds(t, n, stride=T), :].astype(BF)).astype(BF))
        h = stack(hs)
        kr = mm(h, wk_ref[...])
        rk = lax.rsqrt(means(kr * kr) + EPS)
        ku = kr * rk
        v = mm(h, wv_ref[...]).astype(BF)
        w = jnp.exp(c * mm_nt(ku.astype(BF), pu_b))
        wb = w.astype(BF)
        for j in range(GROUP):
            own = slice(j * n, (j + 1) * n)
            p = chunk * GROUP + j
            num1[p] = mm_tn(wb[own], v[own]).reshape(NX, HALVES, KH, D)
            dn[p, :, 0:K] = jnp.sum(w[own], axis=0, keepdims=True)
            hid[p] = h[own]
            kunit[p] = ku[own]
            kscale[p] = rk[own]
            vals[p] = v[own]
            wexp[p] = w[own]

        @pl.when(step == 0)
        def _():
            pl.semaphore_wait(barrier, NZ - 1 + R * NX - 1)

        mine = pl.ds(chunk * GROUP, GROUP)
        for d in range(1, NX):
            start(dn.at[mine], db.at[d - 1, mine], send.at[8], den_r.at[chunk], dev(xpeers[d - 1], z, y, core))
        for k in reversed(range(per_chunk)):
            send_columns(chunk * per_chunk + k, 0, num1, xb1, 0)
        return 0

    lax.fori_loop(0, chunks, first_loop, 0)
    for h in range(1, HALVES):
        for g in reversed(range(T // SENT)):
            send_columns(g, h, num1, xb1, 0)

    loads[6].wait()
    loads[7].wait()
    rows[...] = cot_ref[...].reshape(n * T, D).astype(F32)

    def cot_loop(chunk, _):
        cs = []
        for j in range(GROUP):
            cs.append(rows[pl.ds(step_at(chunk, j), n, stride=T), :].astype(BF))
        d = mm_nt(stack(cs), wo_ref[...]).astype(BF)
        qr = mm(stack([hid[chunk * GROUP + j] for j in range(GROUP)]), wq_ref[...])
        rq = lax.rsqrt(means(qr * qr) + EPS)
        qu = qr * rq
        for j in range(GROUP):
            own = slice(j * n, (j + 1) * n)
            p = chunk * GROUP + j
            cott[p] = cs[j]
            dnorm[p] = d[own]
            qscale[p] = rq[own]
            qunit[p] = qu[own]
        return 0

    lax.fori_loop(0, chunks, cot_loop, 0)
    for chunk in reversed(range(chunks)):
        den_to_owner(chunk)
        for g in reversed(range(chunk * per_chunk, (chunk + 1) * per_chunk)):
            to_owner(g, 0, num1, xb1, zs1, zb1, 0)
    for h in range(1, HALVES):
        for g in reversed(range(T // SENT)):
            to_owner(g, h, num1, xb1, zs1, zb1, 0)

    wait(dzb.at[pl.ds(1, NZ - 1)], den_z)
    den_row = jnp.sum(dzb[...], axis=0)
    dg[0] = den_row
    at = lax.broadcasted_iota(jnp.int32, (KC, D), 1) == lax.broadcasted_iota(jnp.int32, (KC, D), 0) + x * KC
    den_col = jnp.sum(jnp.where(at, den_row, 0.0), axis=1, keepdims=True)
    for h in range(HALVES):
        wait(zb1.at[h, pl.ds(1, NZ - 1)], zs_r.at[0, h])
        gs[0, x, h] = jnp.sum(zb1[h], axis=0) / den_col[h * KH:(h + 1) * KH]
        to_z(gs, h, 0)
    for d in range(1, NZ):
        start(dg.at[0], dg.at[position(NZ - d)], send.at[10], den_g, dev(x, zpeers[d - 1], y, core))

    acc_q[...] = jnp.zeros_like(acc_q)
    acc_o[...] = jnp.zeros_like(acc_o)
    acc_kv[...] = jnp.zeros_like(acc_kv)
    acc_p[...] = jnp.zeros_like(acc_p)

    def second_loop(chunk, _):
        gathered(chunk, gs, 0)
        ps = [chunk * GROUP + j for j in range(GROUP)]
        owns = [slice(j * n, (j + 1) * n) for j in range(GROUP)]
        keys = [slice(j * K, (j + 1) * K) for j in range(GROUP)]
        s = stack([gs[p].reshape(K, D) for p in ps])
        s_b = s.astype(BF)
        rs = lax.rsqrt(means(s * s) + EPS)
        su = s * rs
        su_b = su.astype(BF)
        qu = stack([qunit[p] for p in ps])
        qu_b = qu.astype(BF)
        e = jnp.exp(c * stack([mm_nt(qu_b[o], su_b[k]) for o, k in zip(owns, keys)]))
        e_b = e.astype(BF)
        mixed = stack([mm(e_b[o], s_b[k]) for o, k in zip(owns, keys)])
        inv = 1.0 / mm(e_b, ones[0:K])
        dy = stack([dnorm[p] for p in ps]).astype(F32)
        rb = lax.rsqrt(means(mixed * mixed) * (inv * inv) + EPS)
        scale = rb * inv
        bn = mixed * scale
        normed = bn.astype(BF)
        dbl_b = (rb * (dy - bn * (scale * means(dy * mixed)))).astype(BF)
        a = e * inv[:, 0:K]
        a_b = a.astype(BF)
        ada = a * stack([mm_nt(dbl_b[o], s_b[k]) for o, k in zip(owns, keys)])
        ds_b = (c * (ada - a * mm(ada.astype(BF), ones[0:K, 0:K]))).astype(BF)
        dsu = stack([mm_tn(ds_b[o], qu_b[o]) for o in owns])
        dsum = stack([mm_tn(a_b[o], dbl_b[o]) for o in owns])
        dsum = dsum + rs * (dsu - su * means(dsu * su))
        for j, p in enumerate(ps):
            num2[p] = dsum[keys[j]].reshape(NX, HALVES, KH, D)
        for h in range(HALVES):
            for k in range(per_chunk):
                send_columns(chunk * per_chunk + k, h, num2, xb2, 1)
        dqu = stack([mm(ds_b[o], su_b[k]) for o, k in zip(owns, keys)])
        rq = stack([qscale[p] for p in ps])
        dq = (rq * (dqu - qu * means(dqu * qu))).astype(BF)
        h = stack([hid[p] for p in ps])
        ct = stack([cott[p] for p in ps])
        lo = h.astype(F32) + mm(normed, wo_ref[...])
        part = ct.astype(F32) + mm_nt(dq, wq_ref[...])
        acc_o[...] += mm_tn(normed, ct)
        acc_q[...] += mm_tn(h, dq)
        for j, p in enumerate(ps):
            rows[pl.ds(step_at(chunk, j), n, stride=T), :] = lo[owns[j]]
            pre[p] = part[owns[j]]
        return 0

    gather(gs, 0)
    lax.fori_loop(0, chunks, second_loop, 0)
    for chunk in range(chunks):
        for h in range(HALVES):
            for k in range(per_chunk):
                to_owner(chunk * per_chunk + k, h, num2, xb2, zs2, zb2, 1)

    half = NX // 2
    g_e[:, 0:half] = acc_q[...].reshape(R, half, RX, D)
    g_e[:, half:NX] = acc_o[...].reshape(R, half, RX, D)

    def to_rows(g, t_buf, k):
        for dr, dx in plane:
            px, pr = lax.rem(x + dx, NX), lax.rem(r + dr, R)
            start(g.at[pr, px], t_buf.at[dr * NX + dx], w_send.at[k], w_r.at[k], dev_r(px, pr))
        t_buf[0] = g[r, x]

    def along_z(t_buf, z_buf, k):
        wait(t_buf.at[pl.ds(1, R * NX - 1)], w_r.at[k])
        z_buf[z] = jnp.sum(t_buf[...], axis=0)
        for d in range(1, NZ):
            start(z_buf.at[z], z_buf.at[z], w_send.at[k + 1], w_r.at[k + 1], dev(x, zpeers[d - 1], y, core))

    def along_x(z_buf, f_buf, k):
        wait(z_buf.at[pl.ds(0, NZ - 1)], w_r.at[k + 1])
        f_buf[x] = jnp.sum(z_buf[...], axis=0)
        for d in range(1, NX):
            start(f_buf.at[x], f_buf.at[x], w_send.at[k + 2], w_r.at[k + 2], dev(xpeers[d - 1], z, y, core))

    to_rows(g_e, t_e, 0)
    lo_ref[...] = rows[...].astype(BF).reshape(n, T, D)

    wait(dg.at[pl.ds(0, NZ - 1)], den_g)
    for h in range(HALVES):
        wait(zb2.at[h, pl.ds(1, NZ - 1)], zs_r.at[1, h])
        gd[0, x, h] = jnp.sum(zb2[h], axis=0)
        to_z(gd, h, 1)
    along_z(t_e, z_e, 0)

    w_kv = jnp.concatenate([wk_ref[...], wv_ref[...]], axis=1)
    minus = jnp.full((n, D), -1.0, BF)

    def third_loop(chunk, _):
        gathered(chunk, gd, 1)
        ps = [chunk * GROUP + j for j in range(GROUP)]
        owns = [slice(j * n, (j + 1) * n) for j in range(GROUP)]
        wps, us, dvs = [], [], []
        for p in ps:
            dsum = gd[p].reshape(K, D)
            d_b = dsum.astype(BF)
            both = jnp.concatenate([d_b, (dsum * gs[p].reshape(K, D)).astype(BF)], axis=1)
            wp = wexp[p] * (1.0 / dg[p][:, 0:K])
            wps.append(wp)
            us.append(mm_nt(jnp.concatenate([vals[p], minus], axis=1), both))
            dvs.append(mm(wp.astype(BF), d_b).astype(BF))
        ds_b = (c * (stack(wps) * stack(us))).astype(BF)
        ku = stack([kunit[p] for p in ps])
        rk = stack([kscale[p] for p in ps])
        h = stack([hid[p] for p in ps])
        dku = mm(ds_b, pu_b)
        dk = (rk * (dku - ku * means(dku * ku))).astype(BF)
        dkv = jnp.concatenate([dk, stack(dvs)], axis=1)
        acc_p[...] += mm_tn(ds_b, ku.astype(BF))
        acc_kv[...] += mm_tn(h, dkv)
        dh = mm_nt(dkv, w_kv)
        for j, p in enumerate(ps):
            t = step_at(chunk, j)
            rows[pl.ds(t, n, stride=T), :] = mm(mask_of(t), (pre[p] + dh[owns[j]]).astype(BF))
        return 0

    gather(gd, 1)
    lax.fori_loop(0, chunks, third_loop, 0)

    g_l[:, 0:half] = acc_kv[:, 0:D].reshape(R, half, RX, D)
    g_l[:, half:NX] = acc_kv[:, D:2 * D].reshape(R, half, RX, D)
    g_p[...] = acc_p[...].reshape(R, RP, D)
    to_rows(g_l, t_l, 3)
    for dr in range(R):
        pr = lax.rem(r + dr, R)
        px = lax.rem(pr, NX)
        dx = lax.rem(px - x + NX, NX)
        if dr:
            start(g_p.at[pr], t_p.at[dr * NX + dx], w_send.at[6], w_r.at[6], dev_r(px, pr))
        else:
            @pl.when(dx == 0)
            def _():
                t_p[0] = g_p[r]

            @pl.when(dx != 0)
            def _():
                start(g_p.at[r], t_p.at[dx], w_send.at[9], w_r.at[6], dev_r(px, r))
    meets = x == lax.rem(r, NX)
    along_x(z_e, f_e, 0)
    gi_ref[...] = rows[...].astype(BF).reshape(n, T, D)
    along_z(t_l, z_l, 3)

    @pl.when(meets)
    def _():
        along_z(t_p, z_p, 6)

    along_x(z_l, f_l, 3)

    @pl.when(meets)
    def _():
        wait(z_p.at[pl.ds(0, NZ - 1)], w_r.at[7])
        dpu = jnp.sum(z_p[...], axis=0)
        prow = proj_ref[pl.ds(pl.multiple_of(r * RP, RP), RP), :]
        rp = row_scale(prow)
        pun = prow * rp
        f_p[...] = rp * (dpu - pun * row_mean(dpu * pun))
        for d in range(1, NX):
            start(f_p, f_p, w_send.at[8], w_r.at[8], dev(xpeers[d - 1], z, y, core))

    wait(f_e.at[pl.ds(0, NX - 1)], w_r.at[2])
    final = f_e[...].reshape(2 * RG, D)
    gq_ref[...] = final[0:RG]
    go_ref[...] = final[RG:2 * RG]
    wait(f_l.at[pl.ds(0, NX - 1)], w_r.at[5])
    final = f_l[...].reshape(2 * RG, D)
    gk_ref[...] = final[0:RG]
    gv_ref[...] = final[RG:2 * RG]

    @pl.when(jnp.logical_not(meets))
    def _():
        wait(f_p, w_r.at[8])

    gp_ref[...] = f_p[...]

    wait(xb1, send.at[0])
    wait(zb1.at[:, pl.ds(1, NZ - 1)], send.at[1])
    wait(xb2, send.at[2])
    wait(zb2.at[:, pl.ds(1, NZ - 1)], send.at[3])
    wait(xb1, send.at[4])
    wait(zb1.at[:, pl.ds(1, NZ - 1)], send.at[5])
    wait(xb2, send.at[6])
    wait(zb2.at[:, pl.ds(1, NZ - 1)], send.at[7])
    wait(db, send.at[8])
    wait(dzb.at[pl.ds(1, NZ - 1)], send.at[9])
    wait(dzb.at[pl.ds(1, NZ - 1)], send.at[10])
    for k, t_buf, z_buf, f_buf in ((0, t_e, z_e, f_e), (3, t_l, z_l, f_l)):
        wait(t_buf.at[pl.ds(1, R * NX - 1)], w_send.at[k])
        wait(z_buf.at[pl.ds(0, NZ - 1)], w_send.at[k + 1])
        wait(f_buf.at[pl.ds(0, NX - 1)], w_send.at[k + 2])
    wait(g_p.at[pl.ds(0, R - 1)], w_send.at[6])

    @pl.when(jnp.logical_not(meets))
    def _():
        wait(f_p, w_send.at[9])

    @pl.when(meets)
    def _():
        wait(z_p.at[pl.ds(0, NZ - 1)], w_send.at[7])
        wait(t_p.at[pl.ds(0, NX - 1)], w_send.at[8])


def hand_out(*refs):
    sem = refs[-1]
    copies = [pltpu.make_async_copy(refs[i], refs[i + 7], sem.at[i]) for i in range(7)]
    for copy in copies:
        copy.start()
    for copy in copies:
        copy.wait()


def per_device(dims, inputs, mask, projector, w_key, w_value, w_query, w_out, cotangent):
    NX, NZ, NY, NC, n, T, K, D = dims
    R = NY * NC
    KH = K // NX // HALVES
    RG, RP = D // R, K // R
    RX = 2 * RG // NX
    hbm = pl.BlockSpec(memory_space=pltpu.HBM)
    vm = pl.BlockSpec(memory_space=pltpu.VMEM)
    steps = jax.ShapeDtypeStruct((n, T, D), BF)
    part = jax.ShapeDtypeStruct((RG, D), F32)
    operands = [
        pltpu.with_memory_space_constraint(a, pltpu.HBM)
        for a in (inputs, jnp.swapaxes(mask, 0, 1), projector, w_key, w_value, w_query, w_out, cotangent)
    ]
    lo, gi, gp, gk, gv, gq, go = pl.pallas_call(
        functools.partial(kernel, dims),
        out_shape=(steps, steps, jax.ShapeDtypeStruct((RP, D), F32), part, part, part, part),
        in_specs=[hbm] * 8,
        out_specs=(vm,) * 7,
        scratch_shapes=[
            pltpu.VMEM((n, T, D), BF),
            pltpu.VMEM((T, n), jnp.int32),
            pltpu.VMEM((K, D), F32),
            pltpu.VMEM((D, D), BF),
            pltpu.VMEM((D, D), BF),
            pltpu.VMEM((D, D), BF),
            pltpu.VMEM((D, D), BF),
            pltpu.VMEM((n, T, D), BF),
            pltpu.VMEM((n * T, D), F32),
            pltpu.VMEM((T, n, D), BF),
            pltpu.VMEM((T, n, D), F32),
            pltpu.VMEM((T, n, D), F32),
            pltpu.VMEM((T, n, D), BF),
            pltpu.VMEM((T, n, D), F32),
            pltpu.VMEM((T, n, D), F32),
            pltpu.VMEM((T, n, D), BF),
            pltpu.VMEM((T, n, D), BF),
            pltpu.VMEM((T, n, K), F32),
            pltpu.VMEM((T, n, D), F32),
            pltpu.VMEM((T, NX, HALVES, KH, D), F32),
            pltpu.VMEM((T, HALVES, NX - 1, KH, D), F32),
            pltpu.VMEM((T, HALVES, KH, D), F32),
            pltpu.VMEM((HALVES, NZ, KH, D), F32),
            pltpu.VMEM((T, NX, HALVES, KH, D), F32),
            pltpu.VMEM((T, NX, HALVES, KH, D), F32),
            pltpu.VMEM((T, HALVES, NX - 1, KH, D), F32),
            pltpu.VMEM((T, HALVES, KH, D), F32),
            pltpu.VMEM((HALVES, NZ, KH, D), F32),
            pltpu.VMEM((T, NX, HALVES, KH, D), F32),
            pltpu.VMEM((T, 1, D), F32),
            pltpu.VMEM((NX - 1, T, 1, D), F32),
            pltpu.VMEM((T, 1, D), F32),
            pltpu.VMEM((NZ, 1, D), F32),
            pltpu.VMEM((T, 1, D), F32),
            pltpu.VMEM((K, D), F32),
            pltpu.VMEM((D, 2 * D), F32),
            pltpu.VMEM((D, D), F32),
            pltpu.VMEM((D, D), F32),
            pltpu.VMEM((R, NX, RX, D), F32),
            pltpu.VMEM((R * NX, RX, D), F32),
            pltpu.VMEM((NZ, RX, D), F32),
            pltpu.VMEM((NX, RX, D), F32),
            pltpu.VMEM((R, NX, RX, D), F32),
            pltpu.VMEM((R * NX, RX, D), F32),
            pltpu.VMEM((NZ, RX, D), F32),
            pltpu.VMEM((NX, RX, D), F32),
            pltpu.VMEM((R, RP, D), F32),
            pltpu.VMEM((R * NX, RP, D), F32),
            pltpu.VMEM((NZ, RP, D), F32),
            pltpu.VMEM((RP, D), F32),
            pltpu.SemaphoreType.DMA((8,)),
            pltpu.SemaphoreType.DMA((2, HALVES, T // SENT)),
            pltpu.SemaphoreType.DMA((2, HALVES)),
            pltpu.SemaphoreType.DMA((2, HALVES, T // SENT)),
            pltpu.SemaphoreType.DMA((2, HALVES, T // SENT)),
            pltpu.SemaphoreType.DMA((T // GROUP,)),
            pltpu.SemaphoreType.DMA,
            pltpu.SemaphoreType.DMA,
            pltpu.SemaphoreType.DMA((9,)),
            pltpu.SemaphoreType.DMA((11,)),
            pltpu.SemaphoreType.DMA((10,)),
        ],
        compiler_params=pltpu.CompilerParams(
            collective_id=0, has_side_effects=True, vmem_limit_bytes=48 << 20
        ),
    )(*operands)
    return tuple(
        pl.pallas_call(
            hand_out,
            out_shape=tuple(jax.ShapeDtypeStruct(a.shape, a.dtype) for a in (lo, gi, gp, gk, gv, gq, go)),
            in_specs=[vm] * 7,
            out_specs=(hbm,) * 7,
            scratch_shapes=[pltpu.SemaphoreType.DMA((7,))],
            compiler_params=pltpu.CompilerParams(vmem_limit_bytes=4 << 20),
        )(lo, gi, gp, gk, gv, gq, go)
    )


def build(torus, n, T, K, D):
    dims = tuple(torus.shape[a] for a in AXES) + (n, T, K, D)
    in_specs = (P(SENSOR, TIME, None), P(SENSOR, TIME), P(), P(), P(), P(), P(), P(SENSOR, TIME, None))
    rows = P(TIME, None)
    out_specs = (P(SENSOR, TIME, None), P(SENSOR, TIME, None), rows, rows, rows, rows, rows)
    return jax.shard_map(
        functools.partial(per_device, dims), mesh=torus, in_specs=in_specs, out_specs=out_specs, check_vma=False
    )


def solution(mesh):
    torus = Mesh(mesh.devices.reshape(4, 16, 4, 2), AXES)
    return build(torus, 4096 // 64, 128 // 8, 64, 128)
```

```python
import functools

import jax
import jax.numpy as jnp
from jax import lax
from jax.experimental import pallas as pl
from jax.experimental.pallas import tpu as pltpu
from jax.sharding import Mesh
from jax.sharding import PartitionSpec as P

AXES = ("sx", "sz", "ty", "tc")
SENSOR = ("sx", "sz")
TIME = ("ty", "tc")
MESH_ID = pl.DeviceIdType.MESH
SHARPNESS = 12.0
EPS = 1e-06
GROUP = 4
SENT = 4
HALVES = 2
BF = jnp.bfloat16
F32 = jnp.float32


def mm(a, b):
    return lax.dot_general(a, b, (((1,), (0,)), ((), ())), preferred_element_type=F32)


def mm_nt(a, b):
    return lax.dot_general(a, b, (((1,), (1,)), ((), ())), preferred_element_type=F32)


def mm_tn(a, b):
    return lax.dot_general(a, b, (((0,), (0,)), ((), ())), preferred_element_type=F32)


def row_scale(v):
    return lax.rsqrt(jnp.mean(v * v, axis=-1, keepdims=True) + EPS)


def row_mean(v):
    return jnp.mean(v, axis=-1, keepdims=True)


def stack(parts):
    return jnp.concatenate(parts, axis=0)


def kernel(
    dims,
    x_hbm, mask_hbm, proj_hbm, wk_hbm, wv_hbm, wq_hbm, wo_hbm, cot_hbm,
    lo_ref, gi_ref, gp_ref, gk_ref, gv_ref, gq_ref, go_ref,
    x_ref, mask_ref, proj_ref, wk_ref, wv_ref, wq_ref, wo_ref, cot_ref,
    rows, hid, kunit, kscale, vals, qunit, qscale, cott, dnorm, wexp, pre, norm, dsoft, sunit,
    num1, xb1, zs1, zb1, gs,
    num2, xb2, zs2, zb2, gd,
    dn, db, dz, dzb, dg,
    acc_p, acc_kv, acc_q, acc_o,
    g_e, t_e, z_e, f_e, g_l, t_l, z_l, f_l, g_p, t_p, z_p, f_p,
    in_s, xs_r, zs_r, ag_r, xag_r, den_r, den_z, den_g, w_r, send, w_send,
):
    NX, NZ, NY, NC, n, T, K, D = dims
    KC = K // NX
    KH = KC // HALVES
    R = NY * NC
    RG, RP = D // R, K // R
    RX = 2 * RG // NX
    c = SHARPNESS / D
    x, z, y, core = [lax.axis_index(a) for a in AXES]
    r = y * NC + core

    def dev(ax, az, ay, ac):
        return (ax, az, ay, ac)

    def dev_r(ax, p):
        return (ax, z, lax.div(p, NC), lax.rem(p, NC))

    xpeers = [lax.rem(x + d, NX) for d in range(1, NX)]
    zpeers = [lax.rem(z + d, NZ) for d in range(1, NZ)]
    far_z = sorted(range(1, NZ), key=lambda d: -min(d, NZ - d))
    plane = [(dr, dx) for dr in range(R) for dx in range(NX) if dr or dx]
    plane.sort(key=lambda o: -(min(o[0], R - o[0]) + NC * min(o[1], NX - o[1])))

    loads = [
        pltpu.make_async_copy(a, b, in_s.at[i])
        for i, (a, b) in enumerate([
            (x_hbm, x_ref), (mask_hbm, mask_ref), (proj_hbm, proj_ref), (wk_hbm, wk_ref), (wv_hbm, wv_ref),
            (wq_hbm, wq_ref), (wo_hbm, wo_ref), (cot_hbm, cot_ref),
        ])
    ]
    for load in loads:
        load.start()

    barrier = pltpu.get_barrier_semaphore()
    for p in zpeers:
        pl.semaphore_signal(barrier, inc=1, device_id=dev(x, p, y, core), device_id_type=MESH_ID)
    for dr, dx in plane:
        pl.semaphore_signal(
            barrier, inc=1, device_id=dev_r(lax.rem(x + dx, NX), lax.rem(r + dr, R)), device_id_type=MESH_ID
        )

    def start(src, dst, s_sem, r_sem, device):
        pltpu.make_async_remote_copy(
            src_ref=src, dst_ref=dst, send_sem=s_sem, recv_sem=r_sem, device_id=device, device_id_type=MESH_ID
        ).start()

    def wait(ref, sem):
        pltpu.make_async_copy(ref, ref, sem).wait()

    def step_at(chunk, j):
        ahead = GROUP // 2 * chunk + (j + 1) // 2
        return lax.rem(z + (T - ahead if j % 2 else ahead), T)

    def position(off):
        return 2 * off if off < T - off else 2 * (T - off) - 1

    chunks = T // GROUP
    ones = jnp.ones((D, D), BF)
    diagonal = lax.broadcasted_iota(jnp.int32, (n, n), 0) == lax.broadcasted_iota(jnp.int32, (n, n), 1)

    def mask_of(t):
        return jnp.where(diagonal, mask_ref[pl.ds(t, 1), :].astype(F32), 0.0).astype(BF)

    def means(v):
        return mm(v.astype(BF), ones) * (1.0 / D)

    dn[...] = jnp.zeros_like(dn)
    for load in loads[:6]:
        load.wait()
    proj = proj_ref[...]
    punit = proj * row_scale(proj)
    pu_b = punit.astype(BF)

    rows[...] = x_ref[...].reshape(n * T, D).astype(F32)

    def send_columns(g, h, num, xb, phase):
        some = pl.ds(g * SENT, SENT)
        for d in range(1, NX):
            start(num.at[some, xpeers[d - 1], h], xb.at[some, h, d - 1], send.at[2 * phase], xs_r.at[phase, h, g],
                  dev(xpeers[d - 1], z, y, core))

    def to_owner(g, h, num, xb, zs, zb, phase):
        wait(xb.at[pl.ds(g * SENT, SENT), h], xs_r.at[phase, h, g])
        for k in range(SENT):
            at = g * SENT + k
            total = num[at, x, h]
            for d in range(1, NX):
                total = total + xb[at, h, d - 1]
            if at == 0:
                zb[h, 0] = total
            else:
                zs[at, h] = total
                off = T - (at + 1) // 2 if at % 2 else at // 2
                start(zs.at[at, h], zb.at[h, off], send.at[2 * phase + 1], zs_r.at[phase, h],
                      dev(x, zpeers[off - 1], y, core))

    def den_to_owner(chunk):
        mine = pl.ds(chunk * GROUP, GROUP)
        wait(db.at[pl.ds(0, NX - 1), mine], den_r.at[chunk])
        total = dn[mine]
        for d in range(1, NX):
            total = total + db[d - 1, mine]
        dz[mine] = total
        for j in range(GROUP):
            at = chunk * GROUP + j
            off = T - (at + 1) // 2 if at % 2 else at // 2
            if at == 0:
                dzb[0] = total[0]
            else:
                start(dz.at[at], dzb.at[off], send.at[9], den_z, dev(x, zpeers[off - 1], y, core))

    def to_z(g, h, phase):
        for d in far_z:
            at = position(NZ - d)
            start(g.at[0, x, h], g.at[at, x, h], send.at[5 + 2 * phase], ag_r.at[phase, h, at // SENT],
                  dev(x, zpeers[d - 1], y, core))

    def forward(k, h, g, phase):
        some = pl.ds(k * SENT, SENT)
        came = some if k else pl.ds(1, SENT - 1)
        wait(g.at[came, x, h], ag_r.at[phase, h, k])
        for d in range(1, NX):
            start(g.at[some, x, h], g.at[some, x, h], send.at[4 + 2 * phase], xag_r.at[phase, h, k],
                  dev(xpeers[d - 1], z, y, core))

    def gather(g, phase):
        units = [(k, h) for h in range(HALVES) for k in range(T // SENT)]
        if phase == 0:
            units.sort(key=lambda u: (u[1], -u[0]))
        for k, h in units:
            forward(k, h, g, phase)

    def gathered(chunk, g, phase):
        for k in range(GROUP // SENT):
            p = chunk * (GROUP // SENT) + k
            for h in range(HALVES):
                wait(g.at[pl.ds(p * SENT, SENT), pl.ds(0, NX - 1), h], xag_r.at[phase, h, p])

    per_chunk = GROUP // SENT

    def first_loop(step, _):
        chunk = chunks - 1 - step
        ts = [step_at(chunk, j) for j in range(GROUP)]
        hs = []
        for j, t in enumerate(ts):
            hs.append(mm(mask_of(t), rows[pl.ds(t, n, stride=T), :].astype(BF)).astype(BF))
        h = stack(hs)
        kr = mm(h, wk_ref[...])
        rk = lax.rsqrt(means(kr * kr) + EPS)
        ku = kr * rk
        v = mm(h, wv_ref[...]).astype(BF)
        w = jnp.exp(c * mm_nt(ku.astype(BF), pu_b))
        wb = w.astype(BF)
        for j in range(GROUP):
            own = slice(j * n, (j + 1) * n)
            p = chunk * GROUP + j
            num1[p] = mm_tn(wb[own], v[own]).reshape(NX, HALVES, KH, D)
            dn[p, :, 0:K] = jnp.sum(w[own], axis=0, keepdims=True)
            hid[p] = h[own]
            kunit[p] = ku[own]
            kscale[p] = rk[own]
            vals[p] = v[own]
            wexp[p] = w[own]

        @pl.when(step == 0)
        def _():
            pl.semaphore_wait(barrier, NZ - 1 + R * NX - 1)

        mine = pl.ds(chunk * GROUP, GROUP)
        for d in range(1, NX):
            start(dn.at[mine], db.at[d - 1, mine], send.at[8], den_r.at[chunk], dev(xpeers[d - 1], z, y, core))
        for k in reversed(range(per_chunk)):
            send_columns(chunk * per_chunk + k, 0, num1, xb1, 0)
        return 0

    lax.fori_loop(0, chunks, first_loop, 0)
    for h in range(1, HALVES):
        for g in reversed(range(T // SENT)):
            send_columns(g, h, num1, xb1, 0)

    loads[6].wait()
    loads[7].wait()
    rows[...] = cot_ref[...].reshape(n * T, D).astype(F32)

    def cot_loop(chunk, _):
        cs = []
        for j in range(GROUP):
            cs.append(rows[pl.ds(step_at(chunk, j), n, stride=T), :].astype(BF))
        d = mm_nt(stack(cs), wo_ref[...]).astype(BF)
        qr = mm(stack([hid[chunk * GROUP + j] for j in range(GROUP)]), wq_ref[...])
        rq = lax.rsqrt(means(qr * qr) + EPS)
        qu = qr * rq
        for j in range(GROUP):
            own = slice(j * n, (j + 1) * n)
            p = chunk * GROUP + j
            cott[p] = cs[j]
            dnorm[p] = d[own]
            qscale[p] = rq[own]
            qunit[p] = qu[own]
        return 0

    lax.fori_loop(0, chunks, cot_loop, 0)
    for chunk in reversed(range(chunks)):
        den_to_owner(chunk)
        for g in reversed(range(chunk * per_chunk, (chunk + 1) * per_chunk)):
            to_owner(g, 0, num1, xb1, zs1, zb1, 0)
    for h in range(1, HALVES):
        for g in reversed(range(T // SENT)):
            to_owner(g, h, num1, xb1, zs1, zb1, 0)

    wait(dzb.at[pl.ds(1, NZ - 1)], den_z)
    den_row = jnp.sum(dzb[...], axis=0)
    dg[0] = den_row
    at = lax.broadcasted_iota(jnp.int32, (KC, D), 1) == lax.broadcasted_iota(jnp.int32, (KC, D), 0) + x * KC
    den_col = jnp.sum(jnp.where(at, den_row, 0.0), axis=1, keepdims=True)
    for h in range(HALVES):
        wait(zb1.at[h, pl.ds(1, NZ - 1)], zs_r.at[0, h])
        gs[0, x, h] = jnp.sum(zb1[h], axis=0) / den_col[h * KH:(h + 1) * KH]
        to_z(gs, h, 0)
    for d in far_z:
        start(dg.at[0], dg.at[position(NZ - d)], send.at[10], den_g, dev(x, zpeers[d - 1], y, core))

    acc_q[...] = jnp.zeros_like(acc_q)
    acc_o[...] = jnp.zeros_like(acc_o)
    acc_kv[...] = jnp.zeros_like(acc_kv)
    acc_p[...] = jnp.zeros_like(acc_p)

    def second_loop(step, _):
        chunk = chunks - 1 - step
        gathered(chunk, gs, 0)
        ps = [chunk * GROUP + j for j in range(GROUP)]
        owns = [slice(j * n, (j + 1) * n) for j in range(GROUP)]
        keys = [slice(j * K, (j + 1) * K) for j in range(GROUP)]
        s = stack([gs[p].reshape(K, D) for p in ps])
        s_b = s.astype(BF)
        rs = lax.rsqrt(means(s * s) + EPS)
        su = s * rs
        su_b = su.astype(BF)
        qu = stack([qunit[p] for p in ps])
        qu_b = qu.astype(BF)
        e = jnp.exp(c * stack([mm_nt(qu_b[o], su_b[k]) for o, k in zip(owns, keys)]))
        e_b = e.astype(BF)
        mixed = stack([mm(e_b[o], s_b[k]) for o, k in zip(owns, keys)])
        inv = 1.0 / mm(e_b, ones[0:K])
        dy = stack([dnorm[p] for p in ps]).astype(F32)
        rb = lax.rsqrt(means(mixed * mixed) * (inv * inv) + EPS)
        scale = rb * inv
        bn = mixed * scale
        normed = bn.astype(BF)
        dbl_b = (rb * (dy - bn * (scale * means(dy * mixed)))).astype(BF)
        a = e * inv[:, 0:K]
        a_b = a.astype(BF)
        ada = a * stack([mm_nt(dbl_b[o], s_b[k]) for o, k in zip(owns, keys)])
        ds_b = (c * (ada - a * mm(ada.astype(BF), ones[0:K, 0:K]))).astype(BF)
        dsu = stack([mm_tn(ds_b[o], qu_b[o]) for o in owns])
        dsum = stack([mm_tn(a_b[o], dbl_b[o]) for o in owns])
        dsum = dsum + rs * (dsu - su * means(dsu * su))
        for j, p in enumerate(ps):
            num2[p] = dsum[keys[j]].reshape(NX, HALVES, KH, D)
        for h in range(HALVES):
            for k in range(per_chunk):
                send_columns(chunk * per_chunk + k, h, num2, xb2, 1)
        for j, p in enumerate(ps):
            norm[p] = normed[owns[j]]
            dsoft[p] = ds_b[owns[j]]
            sunit[p] = su_b[keys[j]]
        return 0

    def second_rest(chunk):
        ps = [chunk * GROUP + j for j in range(GROUP)]
        owns = [slice(j * n, (j + 1) * n) for j in range(GROUP)]
        normed = stack([norm[p] for p in ps])
        qu = stack([qunit[p] for p in ps])
        rq = stack([qscale[p] for p in ps])
        dqu = stack([mm(dsoft[p], sunit[p]) for p in ps])
        dq = (rq * (dqu - qu * means(dqu * qu))).astype(BF)
        h = stack([hid[p] for p in ps])
        ct = stack([cott[p] for p in ps])
        lo = h.astype(F32) + mm(normed, wo_ref[...])
        part = ct.astype(F32) + mm_nt(dq, wq_ref[...])
        acc_o[...] += mm_tn(normed, ct)
        acc_q[...] += mm_tn(h, dq)
        for j, p in enumerate(ps):
            rows[pl.ds(step_at(chunk, j), n, stride=T), :] = lo[owns[j]]
            pre[p] = part[owns[j]]

    def second_owner(chunk):
        for h in range(HALVES):
            for k in range(per_chunk):
                to_owner(chunk * per_chunk + k, h, num2, xb2, zs2, zb2, 1)

    gather(gs, 0)
    lax.fori_loop(0, chunks, second_loop, 0)
    late = chunks // 2
    for chunk in reversed(range(late, chunks)):
        second_rest(chunk)
    for chunk in reversed(range(chunks)):
        second_owner(chunk)
    for chunk in reversed(range(late)):
        second_rest(chunk)

    half = NX // 2
    g_e[:, 0:half] = acc_q[...].reshape(R, half, RX, D)
    g_e[:, half:NX] = acc_o[...].reshape(R, half, RX, D)

    def to_rows(g, t_buf, k):
        for dr, dx in plane:
            px, pr = lax.rem(x + dx, NX), lax.rem(r + dr, R)
            start(g.at[pr, px], t_buf.at[dr * NX + dx], w_send.at[k], w_r.at[k], dev_r(px, pr))
        t_buf[0] = g[r, x]

    def along_z(t_buf, z_buf, k):
        wait(t_buf.at[pl.ds(1, R * NX - 1)], w_r.at[k])
        z_buf[z] = jnp.sum(t_buf[...], axis=0)
        for d in far_z:
            start(z_buf.at[z], z_buf.at[z], w_send.at[k + 1], w_r.at[k + 1], dev(x, zpeers[d - 1], y, core))

    def along_x(z_buf, f_buf, k):
        wait(z_buf.at[pl.ds(0, NZ - 1)], w_r.at[k + 1])
        f_buf[x] = jnp.sum(z_buf[...], axis=0)
        for d in range(1, NX):
            start(f_buf.at[x], f_buf.at[x], w_send.at[k + 2], w_r.at[k + 2], dev(xpeers[d - 1], z, y, core))

    to_rows(g_e, t_e, 0)
    lo_ref[...] = rows[...].astype(BF).reshape(n, T, D)

    wait(dg.at[pl.ds(0, NZ - 1)], den_g)
    for h in range(HALVES):
        wait(zb2.at[h, pl.ds(1, NZ - 1)], zs_r.at[1, h])
        gd[0, x, h] = jnp.sum(zb2[h], axis=0)
        to_z(gd, h, 1)

    w_kv = jnp.concatenate([wk_ref[...], wv_ref[...]], axis=1)
    minus = jnp.full((n, D), -1.0, BF)

    def third_loop(chunk, _):
        gathered(chunk, gd, 1)
        ps = [chunk * GROUP + j for j in range(GROUP)]
        owns = [slice(j * n, (j + 1) * n) for j in range(GROUP)]
        wps, us, dvs = [], [], []
        for p in ps:
            dsum = gd[p].reshape(K, D)
            d_b = dsum.astype(BF)
            both = jnp.concatenate([d_b, (dsum * gs[p].reshape(K, D)).astype(BF)], axis=1)
            wp = wexp[p] * (1.0 / dg[p][:, 0:K])
            wps.append(wp)
            us.append(mm_nt(jnp.concatenate([vals[p], minus], axis=1), both))
            dvs.append(mm(wp.astype(BF), d_b).astype(BF))
        ds_b = (c * (stack(wps) * stack(us))).astype(BF)
        ku = stack([kunit[p] for p in ps])
        rk = stack([kscale[p] for p in ps])
        h = stack([hid[p] for p in ps])
        dku = mm(ds_b, pu_b)
        dk = (rk * (dku - ku * means(dku * ku))).astype(BF)
        dkv = jnp.concatenate([dk, stack(dvs)], axis=1)
        acc_p[...] += mm_tn(ds_b, ku.astype(BF))
        acc_kv[...] += mm_tn(h, dkv)
        dh = mm_nt(dkv, w_kv)
        for j, p in enumerate(ps):
            t = step_at(chunk, j)
            rows[pl.ds(t, n, stride=T), :] = mm(mask_of(t), (pre[p] + dh[owns[j]]).astype(BF))
        return 0

    gather(gd, 1)
    along_z(t_e, z_e, 0)
    lax.fori_loop(0, chunks, third_loop, 0)

    g_l[:, 0:half] = acc_kv[:, 0:D].reshape(R, half, RX, D)
    g_l[:, half:NX] = acc_kv[:, D:2 * D].reshape(R, half, RX, D)
    g_p[...] = acc_p[...].reshape(R, RP, D)
    to_rows(g_l, t_l, 3)
    for dr in range(R):
        pr = lax.rem(r + dr, R)
        px = lax.rem(pr, NX)
        dx = lax.rem(px - x + NX, NX)
        if dr:
            start(g_p.at[pr], t_p.at[dr * NX + dx], w_send.at[6], w_r.at[6], dev_r(px, pr))
        else:
            @pl.when(dx == 0)
            def _():
                t_p[0] = g_p[r]

            @pl.when(dx != 0)
            def _():
                start(g_p.at[r], t_p.at[dx], w_send.at[9], w_r.at[6], dev_r(px, r))
    meets = x == lax.rem(r, NX)
    along_x(z_e, f_e, 0)
    gi_ref[...] = rows[...].astype(BF).reshape(n, T, D)
    along_z(t_l, z_l, 3)

    @pl.when(meets)
    def _():
        along_z(t_p, z_p, 6)

    along_x(z_l, f_l, 3)

    @pl.when(meets)
    def _():
        wait(z_p.at[pl.ds(0, NZ - 1)], w_r.at[7])
        dpu = jnp.sum(z_p[...], axis=0)
        prow = proj_ref[pl.ds(pl.multiple_of(r * RP, RP), RP), :]
        rp = row_scale(prow)
        pun = prow * rp
        f_p[...] = rp * (dpu - pun * row_mean(dpu * pun))
        for d in range(1, NX):
            start(f_p, f_p, w_send.at[8], w_r.at[8], dev(xpeers[d - 1], z, y, core))

    wait(f_e.at[pl.ds(0, NX - 1)], w_r.at[2])
    final = f_e[...].reshape(2 * RG, D)
    gq_ref[...] = final[0:RG]
    go_ref[...] = final[RG:2 * RG]
    wait(f_l.at[pl.ds(0, NX - 1)], w_r.at[5])
    final = f_l[...].reshape(2 * RG, D)
    gk_ref[...] = final[0:RG]
    gv_ref[...] = final[RG:2 * RG]

    @pl.when(jnp.logical_not(meets))
    def _():
        wait(f_p, w_r.at[8])

    gp_ref[...] = f_p[...]

    wait(xb1, send.at[0])
    wait(zb1.at[:, pl.ds(1, NZ - 1)], send.at[1])
    wait(xb2, send.at[2])
    wait(zb2.at[:, pl.ds(1, NZ - 1)], send.at[3])
    wait(xb1, send.at[4])
    wait(zb1.at[:, pl.ds(1, NZ - 1)], send.at[5])
    wait(xb2, send.at[6])
    wait(zb2.at[:, pl.ds(1, NZ - 1)], send.at[7])
    wait(db, send.at[8])
    wait(dzb.at[pl.ds(1, NZ - 1)], send.at[9])
    wait(dzb.at[pl.ds(1, NZ - 1)], send.at[10])
    for k, t_buf, z_buf, f_buf in ((0, t_e, z_e, f_e), (3, t_l, z_l, f_l)):
        wait(t_buf.at[pl.ds(1, R * NX - 1)], w_send.at[k])
        wait(z_buf.at[pl.ds(0, NZ - 1)], w_send.at[k + 1])
        wait(f_buf.at[pl.ds(0, NX - 1)], w_send.at[k + 2])
    wait(g_p.at[pl.ds(0, R - 1)], w_send.at[6])

    @pl.when(jnp.logical_not(meets))
    def _():
        wait(f_p, w_send.at[9])

    @pl.when(meets)
    def _():
        wait(z_p.at[pl.ds(0, NZ - 1)], w_send.at[7])
        wait(t_p.at[pl.ds(0, NX - 1)], w_send.at[8])


def hand_out(*refs):
    sem = refs[-1]
    copies = [pltpu.make_async_copy(refs[i], refs[i + 7], sem.at[i]) for i in range(7)]
    for copy in copies:
        copy.start()
    for copy in copies:
        copy.wait()


def per_device(dims, inputs, mask, projector, w_key, w_value, w_query, w_out, cotangent):
    NX, NZ, NY, NC, n, T, K, D = dims
    R = NY * NC
    KH = K // NX // HALVES
    RG, RP = D // R, K // R
    RX = 2 * RG // NX
    hbm = pl.BlockSpec(memory_space=pltpu.HBM)
    vm = pl.BlockSpec(memory_space=pltpu.VMEM)
    steps = jax.ShapeDtypeStruct((n, T, D), BF)
    part = jax.ShapeDtypeStruct((RG, D), F32)
    operands = [
        pltpu.with_memory_space_constraint(a, pltpu.HBM)
        for a in (inputs, jnp.swapaxes(mask, 0, 1), projector, w_key, w_value, w_query, w_out, cotangent)
    ]
    lo, gi, gp, gk, gv, gq, go = pl.pallas_call(
        functools.partial(kernel, dims),
        out_shape=(steps, steps, jax.ShapeDtypeStruct((RP, D), F32), part, part, part, part),
        in_specs=[hbm] * 8,
        out_specs=(vm,) * 7,
        scratch_shapes=[
            pltpu.VMEM((n, T, D), BF),
            pltpu.VMEM((T, n), jnp.int32),
            pltpu.VMEM((K, D), F32),
            pltpu.VMEM((D, D), BF),
            pltpu.VMEM((D, D), BF),
            pltpu.VMEM((D, D), BF),
            pltpu.VMEM((D, D), BF),
            pltpu.VMEM((n, T, D), BF),
            pltpu.VMEM((n * T, D), F32),
            pltpu.VMEM((T, n, D), BF),
            pltpu.VMEM((T, n, D), F32),
            pltpu.VMEM((T, n, D), F32),
            pltpu.VMEM((T, n, D), BF),
            pltpu.VMEM((T, n, D), F32),
            pltpu.VMEM((T, n, D), F32),
            pltpu.VMEM((T, n, D), BF),
            pltpu.VMEM((T, n, D), BF),
            pltpu.VMEM((T, n, K), F32),
            pltpu.VMEM((T, n, D), F32),
            pltpu.VMEM((T, n, D), BF),
            pltpu.VMEM((T, n, K), BF),
            pltpu.VMEM((T, K, D), BF),
            pltpu.VMEM((T, NX, HALVES, KH, D), F32),
            pltpu.VMEM((T, HALVES, NX - 1, KH, D), F32),
            pltpu.VMEM((T, HALVES, KH, D), F32),
            pltpu.VMEM((HALVES, NZ, KH, D), F32),
            pltpu.VMEM((T, NX, HALVES, KH, D), F32),
            pltpu.VMEM((T, NX, HALVES, KH, D), F32),
            pltpu.VMEM((T, HALVES, NX - 1, KH, D), F32),
            pltpu.VMEM((T, HALVES, KH, D), F32),
            pltpu.VMEM((HALVES, NZ, KH, D), F32),
            pltpu.VMEM((T, NX, HALVES, KH, D), F32),
            pltpu.VMEM((T, 1, D), F32),
            pltpu.VMEM((NX - 1, T, 1, D), F32),
            pltpu.VMEM((T, 1, D), F32),
            pltpu.VMEM((NZ, 1, D), F32),
            pltpu.VMEM((T, 1, D), F32),
            pltpu.VMEM((K, D), F32),
            pltpu.VMEM((D, 2 * D), F32),
            pltpu.VMEM((D, D), F32),
            pltpu.VMEM((D, D), F32),
            pltpu.VMEM((R, NX, RX, D), F32),
            pltpu.VMEM((R * NX, RX, D), F32),
            pltpu.VMEM((NZ, RX, D), F32),
            pltpu.VMEM((NX, RX, D), F32),
            pltpu.VMEM((R, NX, RX, D), F32),
            pltpu.VMEM((R * NX, RX, D), F32),
            pltpu.VMEM((NZ, RX, D), F32),
            pltpu.VMEM((NX, RX, D), F32),
            pltpu.VMEM((R, RP, D), F32),
            pltpu.VMEM((R * NX, RP, D), F32),
            pltpu.VMEM((NZ, RP, D), F32),
            pltpu.VMEM((RP, D), F32),
            pltpu.SemaphoreType.DMA((8,)),
            pltpu.SemaphoreType.DMA((2, HALVES, T // SENT)),
            pltpu.SemaphoreType.DMA((2, HALVES)),
            pltpu.SemaphoreType.DMA((2, HALVES, T // SENT)),
            pltpu.SemaphoreType.DMA((2, HALVES, T // SENT)),
            pltpu.SemaphoreType.DMA((T // GROUP,)),
            pltpu.SemaphoreType.DMA,
            pltpu.SemaphoreType.DMA,
            pltpu.SemaphoreType.DMA((9,)),
            pltpu.SemaphoreType.DMA((11,)),
            pltpu.SemaphoreType.DMA((10,)),
        ],
        compiler_params=pltpu.CompilerParams(
            collective_id=0, has_side_effects=True, vmem_limit_bytes=48 << 20
        ),
    )(*operands)
    return tuple(
        pl.pallas_call(
            hand_out,
            out_shape=tuple(jax.ShapeDtypeStruct(a.shape, a.dtype) for a in (lo, gi, gp, gk, gv, gq, go)),
            in_specs=[vm] * 7,
            out_specs=(hbm,) * 7,
            scratch_shapes=[pltpu.SemaphoreType.DMA((7,))],
            compiler_params=pltpu.CompilerParams(vmem_limit_bytes=4 << 20),
        )(lo, gi, gp, gk, gv, gq, go)
    )


def build(torus, n, T, K, D):
    dims = tuple(torus.shape[a] for a in AXES) + (n, T, K, D)
    in_specs = (P(SENSOR, TIME, None), P(SENSOR, TIME), P(), P(), P(), P(), P(), P(SENSOR, TIME, None))
    rows = P(TIME, None)
    out_specs = (P(SENSOR, TIME, None), P(SENSOR, TIME, None), rows, rows, rows, rows, rows)
    return jax.shard_map(
        functools.partial(per_device, dims), mesh=torus, in_specs=in_specs, out_specs=out_specs, check_vma=False
    )


def solution(mesh):
    torus = Mesh(mesh.devices.reshape(4, 16, 4, 2), AXES)
    return build(torus, 4096 // 64, 128 // 8, 64, 128)
```

```python
import functools

import jax
import jax.numpy as jnp
from jax import lax
from jax.experimental import pallas as pl
from jax.experimental.pallas import tpu as pltpu
from jax.sharding import Mesh
from jax.sharding import PartitionSpec as P

AXES = ("sx", "sz", "ty", "tc")
SENSOR = ("sx", "sz")
TIME = ("ty", "tc")
MESH_ID = pl.DeviceIdType.MESH
SHARPNESS = 12.0
EPS = 1e-06
GROUP = 4
SENT = 4
HALVES = 2
BF = jnp.bfloat16
F32 = jnp.float32


def mm(a, b):
    return lax.dot_general(a, b, (((1,), (0,)), ((), ())), preferred_element_type=F32)


def mm_nt(a, b):
    return lax.dot_general(a, b, (((1,), (1,)), ((), ())), preferred_element_type=F32)


def mm_tn(a, b):
    return lax.dot_general(a, b, (((0,), (0,)), ((), ())), preferred_element_type=F32)


def row_scale(v):
    return lax.rsqrt(jnp.mean(v * v, axis=-1, keepdims=True) + EPS)


def row_mean(v):
    return jnp.mean(v, axis=-1, keepdims=True)


def stack(parts):
    return jnp.concatenate(parts, axis=0)


def kernel(
    dims,
    x_hbm, mask_hbm, proj_hbm, wk_hbm, wv_hbm, wq_hbm, wo_hbm, cot_hbm,
    lo_ref, gi_ref, gp_ref, gk_ref, gv_ref, gq_ref, go_ref,
    x_ref, mask_ref, proj_ref, wk_ref, wv_ref, wq_ref, wo_ref, cot_ref,
    rows, hid, kunit, kscale, vals, qunit, qscale, cott, dnorm, wexp, pre, norm, dsoft, sunit,
    num1, xb1, zs1, zb1, gs,
    num2, xb2, zs2, zb2, gd,
    dn, db, dz, dzb, dg,
    acc_p, acc_kv, acc_q, acc_o,
    g_e, t_e, z_e, f_e, g_l, t_l, z_l, f_l, g_p, t_p, z_p, f_p,
    in_s, xs_r, zs_r, ag_r, xag_r, den_r, den_z, den_g, w_r, send, w_send,
):
    NX, NZ, NY, NC, n, T, K, D = dims
    KC = K // NX
    KH = KC // HALVES
    R = NY * NC
    RG, RP = D // R, K // R
    RX = 2 * RG // NX
    c = SHARPNESS / D
    x, z, y, core = [lax.axis_index(a) for a in AXES]
    r = y * NC + core

    def dev(ax, az, ay, ac):
        return (ax, az, ay, ac)

    def dev_r(ax, p):
        return (ax, z, lax.div(p, NC), lax.rem(p, NC))

    xpeers = [lax.rem(x + d, NX) for d in range(1, NX)]
    zpeers = [lax.rem(z + d, NZ) for d in range(1, NZ)]
    far_x = sorted(range(1, NX), key=lambda d: -min(d, NX - d))
    far_z = sorted(range(1, NZ), key=lambda d: -min(d, NZ - d))
    plane = [(dr, dx) for dr in range(R) for dx in range(NX) if dr or dx]
    plane.sort(key=lambda o: -(min(o[0], R - o[0]) + NC * min(o[1], NX - o[1])))

    loads = [
        pltpu.make_async_copy(a, b, in_s.at[i])
        for i, (a, b) in enumerate([
            (x_hbm, x_ref), (mask_hbm, mask_ref), (proj_hbm, proj_ref), (wk_hbm, wk_ref), (wv_hbm, wv_ref),
            (wq_hbm, wq_ref), (wo_hbm, wo_ref), (cot_hbm, cot_ref),
        ])
    ]
    for load in loads:
        load.start()

    barrier = pltpu.get_barrier_semaphore()
    for p in zpeers:
        pl.semaphore_signal(barrier, inc=1, device_id=dev(x, p, y, core), device_id_type=MESH_ID)
    for dr, dx in plane:
        pl.semaphore_signal(
            barrier, inc=1, device_id=dev_r(lax.rem(x + dx, NX), lax.rem(r + dr, R)), device_id_type=MESH_ID
        )

    def start(src, dst, s_sem, r_sem, device):
        pltpu.make_async_remote_copy(
            src_ref=src, dst_ref=dst, send_sem=s_sem, recv_sem=r_sem, device_id=device, device_id_type=MESH_ID
        ).start()

    def wait(ref, sem):
        pltpu.make_async_copy(ref, ref, sem).wait()

    def step_at(chunk, j):
        ahead = GROUP // 2 * chunk + (j + 1) // 2
        return lax.rem(z + (T - ahead if j % 2 else ahead), T)

    def position(off):
        return 2 * off if off < T - off else 2 * (T - off) - 1

    chunks = T // GROUP
    ones = jnp.ones((D, D), BF)
    diagonal = lax.broadcasted_iota(jnp.int32, (n, n), 0) == lax.broadcasted_iota(jnp.int32, (n, n), 1)

    def mask_of(t):
        return jnp.where(diagonal, mask_ref[pl.ds(t, 1), :].astype(F32), 0.0).astype(BF)

    def means(v):
        return mm(v.astype(BF), ones) * (1.0 / D)

    dn[...] = jnp.zeros_like(dn)
    for load in loads[:6]:
        load.wait()
    proj = proj_ref[...]
    punit = proj * row_scale(proj)
    pu_b = punit.astype(BF)

    rows[...] = x_ref[...].reshape(n * T, D).astype(F32)

    def send_columns(g, h, num, xb, phase):
        some = pl.ds(g * SENT, SENT)
        for d in far_x:
            start(num.at[some, xpeers[d - 1], h], xb.at[some, h, d - 1], send.at[2 * phase], xs_r.at[phase, h, g],
                  dev(xpeers[d - 1], z, y, core))

    def to_owner(g, h, num, xb, zs, zb, phase):
        wait(xb.at[pl.ds(g * SENT, SENT), h], xs_r.at[phase, h, g])
        for k in range(SENT):
            at = g * SENT + k
            total = num[at, x, h]
            for d in range(1, NX):
                total = total + xb[at, h, d - 1]
            if at == 0:
                zb[h, 0] = total
            else:
                zs[at, h] = total
                off = T - (at + 1) // 2 if at % 2 else at // 2
                start(zs.at[at, h], zb.at[h, off], send.at[2 * phase + 1], zs_r.at[phase, h],
                      dev(x, zpeers[off - 1], y, core))

    def den_to_owner(chunk):
        mine = pl.ds(chunk * GROUP, GROUP)
        wait(db.at[pl.ds(0, NX - 1), mine], den_r.at[chunk])
        total = dn[mine]
        for d in range(1, NX):
            total = total + db[d - 1, mine]
        dz[mine] = total
        for j in range(GROUP):
            at = chunk * GROUP + j
            off = T - (at + 1) // 2 if at % 2 else at // 2
            if at == 0:
                dzb[0] = total[0]
            else:
                start(dz.at[at], dzb.at[off], send.at[9], den_z, dev(x, zpeers[off - 1], y, core))

    def to_z(g, h, phase):
        for d in far_z:
            at = position(NZ - d)
            start(g.at[0, x, h], g.at[at, x, h], send.at[5 + 2 * phase], ag_r.at[phase, h, at // SENT],
                  dev(x, zpeers[d - 1], y, core))

    def forward(k, h, g, phase):
        some = pl.ds(k * SENT, SENT)
        came = some if k else pl.ds(1, SENT - 1)
        wait(g.at[came, x, h], ag_r.at[phase, h, k])
        for d in far_x:
            start(g.at[some, x, h], g.at[some, x, h], send.at[4 + 2 * phase], xag_r.at[phase, h, k],
                  dev(xpeers[d - 1], z, y, core))

    def gather(g, phase):
        units = [(k, h) for h in range(HALVES) for k in range(T // SENT)]
        if phase == 0:
            units.sort(key=lambda u: (u[1], -u[0]))
        for k, h in units:
            forward(k, h, g, phase)

    def gathered(chunk, g, phase):
        for k in range(GROUP // SENT):
            p = chunk * (GROUP // SENT) + k
            for h in range(HALVES):
                wait(g.at[pl.ds(p * SENT, SENT), pl.ds(0, NX - 1), h], xag_r.at[phase, h, p])

    per_chunk = GROUP // SENT

    def first_loop(step, _):
        chunk = chunks - 1 - step
        ts = [step_at(chunk, j) for j in range(GROUP)]
        hs = []
        for j, t in enumerate(ts):
            hs.append(mm(mask_of(t), rows[pl.ds(t, n, stride=T), :].astype(BF)).astype(BF))
        h = stack(hs)
        kr = mm(h, wk_ref[...])
        rk = lax.rsqrt(means(kr * kr) + EPS)
        ku = kr * rk
        v = mm(h, wv_ref[...]).astype(BF)
        w = jnp.exp(c * mm_nt(ku.astype(BF), pu_b))
        wb = w.astype(BF)
        for j in range(GROUP):
            own = slice(j * n, (j + 1) * n)
            p = chunk * GROUP + j
            num1[p] = mm_tn(wb[own], v[own]).reshape(NX, HALVES, KH, D)
            dn[p, :, 0:K] = jnp.sum(w[own], axis=0, keepdims=True)
            hid[p] = h[own]
            kunit[p] = ku[own]
            kscale[p] = rk[own]
            vals[p] = v[own]
            wexp[p] = w[own]

        @pl.when(step == 0)
        def _():
            pl.semaphore_wait(barrier, NZ - 1 + R * NX - 1)

        mine = pl.ds(chunk * GROUP, GROUP)
        for d in far_x:
            start(dn.at[mine], db.at[d - 1, mine], send.at[8], den_r.at[chunk], dev(xpeers[d - 1], z, y, core))
        for k in reversed(range(per_chunk)):
            send_columns(chunk * per_chunk + k, 0, num1, xb1, 0)
        return 0

    lax.fori_loop(0, chunks, first_loop, 0)
    for h in range(1, HALVES):
        for g in reversed(range(T // SENT)):
            send_columns(g, h, num1, xb1, 0)

    loads[6].wait()
    loads[7].wait()
    rows[...] = cot_ref[...].reshape(n * T, D).astype(F32)

    def cot_loop(chunk, _):
        cs = []
        for j in range(GROUP):
            cs.append(rows[pl.ds(step_at(chunk, j), n, stride=T), :].astype(BF))
        d = mm_nt(stack(cs), wo_ref[...]).astype(BF)
        qr = mm(stack([hid[chunk * GROUP + j] for j in range(GROUP)]), wq_ref[...])
        rq = lax.rsqrt(means(qr * qr) + EPS)
        qu = qr * rq
        for j in range(GROUP):
            own = slice(j * n, (j + 1) * n)
            p = chunk * GROUP + j
            cott[p] = cs[j]
            dnorm[p] = d[own]
            qscale[p] = rq[own]
            qunit[p] = qu[own]
        return 0

    lax.fori_loop(0, chunks, cot_loop, 0)
    for chunk in reversed(range(chunks)):
        den_to_owner(chunk)
        for g in reversed(range(chunk * per_chunk, (chunk + 1) * per_chunk)):
            to_owner(g, 0, num1, xb1, zs1, zb1, 0)
    for h in range(1, HALVES):
        for g in reversed(range(T // SENT)):
            to_owner(g, h, num1, xb1, zs1, zb1, 0)

    wait(dzb.at[pl.ds(1, NZ - 1)], den_z)
    den_row = jnp.sum(dzb[...], axis=0)
    dg[0] = den_row
    at = lax.broadcasted_iota(jnp.int32, (KC, D), 1) == lax.broadcasted_iota(jnp.int32, (KC, D), 0) + x * KC
    den_col = jnp.sum(jnp.where(at, den_row, 0.0), axis=1, keepdims=True)
    for h in range(HALVES):
        wait(zb1.at[h, pl.ds(1, NZ - 1)], zs_r.at[0, h])
        gs[0, x, h] = jnp.sum(zb1[h], axis=0) / den_col[h * KH:(h + 1) * KH]
        to_z(gs, h, 0)
    for d in far_z:
        start(dg.at[0], dg.at[position(NZ - d)], send.at[10], den_g, dev(x, zpeers[d - 1], y, core))

    acc_q[...] = jnp.zeros_like(acc_q)
    acc_o[...] = jnp.zeros_like(acc_o)
    acc_kv[...] = jnp.zeros_like(acc_kv)
    acc_p[...] = jnp.zeros_like(acc_p)

    def second_loop(step, _):
        chunk = chunks - 1 - step
        gathered(chunk, gs, 0)
        ps = [chunk * GROUP + j for j in range(GROUP)]
        owns = [slice(j * n, (j + 1) * n) for j in range(GROUP)]
        keys = [slice(j * K, (j + 1) * K) for j in range(GROUP)]
        s = stack([gs[p].reshape(K, D) for p in ps])
        s_b = s.astype(BF)
        rs = lax.rsqrt(means(s * s) + EPS)
        su = s * rs
        su_b = su.astype(BF)
        qu = stack([qunit[p] for p in ps])
        qu_b = qu.astype(BF)
        e = jnp.exp(c * stack([mm_nt(qu_b[o], su_b[k]) for o, k in zip(owns, keys)]))
        e_b = e.astype(BF)
        mixed = stack([mm(e_b[o], s_b[k]) for o, k in zip(owns, keys)])
        inv = 1.0 / mm(e_b, ones[0:K])
        dy = stack([dnorm[p] for p in ps]).astype(F32)
        rb = lax.rsqrt(means(mixed * mixed) * (inv * inv) + EPS)
        scale = rb * inv
        bn = mixed * scale
        normed = bn.astype(BF)
        dbl_b = (rb * (dy - bn * (scale * means(dy * mixed)))).astype(BF)
        a = e * inv[:, 0:K]
        a_b = a.astype(BF)
        ada = a * stack([mm_nt(dbl_b[o], s_b[k]) for o, k in zip(owns, keys)])
        ds_b = (c * (ada - a * mm(ada.astype(BF), ones[0:K, 0:K]))).astype(BF)
        dsu = stack([mm_tn(ds_b[o], qu_b[o]) for o in owns])
        dsum = stack([mm_tn(a_b[o], dbl_b[o]) for o in owns])
        dsum = dsum + rs * (dsu - su * means(dsu * su))
        for j, p in enumerate(ps):
            num2[p] = dsum[keys[j]].reshape(NX, HALVES, KH, D)
        for h in range(HALVES):
            for k in range(per_chunk):
                send_columns(chunk * per_chunk + k, h, num2, xb2, 1)
        for j, p in enumerate(ps):
            norm[p] = normed[owns[j]]
            dsoft[p] = ds_b[owns[j]]
            sunit[p] = su_b[keys[j]]
        return 0

    def second_rest(chunk):
        ps = [chunk * GROUP + j for j in range(GROUP)]
        owns = [slice(j * n, (j + 1) * n) for j in range(GROUP)]
        normed = stack([norm[p] for p in ps])
        qu = stack([qunit[p] for p in ps])
        rq = stack([qscale[p] for p in ps])
        dqu = stack([mm(dsoft[p], sunit[p]) for p in ps])
        dq = (rq * (dqu - qu * means(dqu * qu))).astype(BF)
        h = stack([hid[p] for p in ps])
        ct = stack([cott[p] for p in ps])
        lo = h.astype(F32) + mm(normed, wo_ref[...])
        part = ct.astype(F32) + mm_nt(dq, wq_ref[...])
        acc_o[...] += mm_tn(normed, ct)
        acc_q[...] += mm_tn(h, dq)
        for j, p in enumerate(ps):
            rows[pl.ds(step_at(chunk, j), n, stride=T), :] = lo[owns[j]]
            pre[p] = part[owns[j]]

    def second_owner(chunk):
        for h in range(HALVES):
            for k in range(per_chunk):
                to_owner(chunk * per_chunk + k, h, num2, xb2, zs2, zb2, 1)

    gather(gs, 0)
    lax.fori_loop(0, chunks, second_loop, 0)
    late = chunks // 2
    for chunk in reversed(range(late, chunks)):
        second_rest(chunk)
    for chunk in reversed(range(chunks)):
        second_owner(chunk)
    for chunk in reversed(range(late)):
        second_rest(chunk)

    half = NX // 2
    g_e[:, 0:half] = acc_q[...].reshape(R, half, RX, D)
    g_e[:, half:NX] = acc_o[...].reshape(R, half, RX, D)

    def to_rows(g, t_buf, k):
        for dr, dx in plane:
            px, pr = lax.rem(x + dx, NX), lax.rem(r + dr, R)
            start(g.at[pr, px], t_buf.at[dr * NX + dx], w_send.at[k], w_r.at[k], dev_r(px, pr))
        t_buf[0] = g[r, x]

    def along_z(t_buf, z_buf, k):
        wait(t_buf.at[pl.ds(1, R * NX - 1)], w_r.at[k])
        z_buf[z] = jnp.sum(t_buf[...], axis=0)
        for d in far_z:
            start(z_buf.at[z], z_buf.at[z], w_send.at[k + 1], w_r.at[k + 1], dev(x, zpeers[d - 1], y, core))

    def along_x(z_buf, f_buf, k):
        wait(z_buf.at[pl.ds(0, NZ - 1)], w_r.at[k + 1])
        f_buf[x] = jnp.sum(z_buf[...], axis=0)
        for d in far_x:
            start(f_buf.at[x], f_buf.at[x], w_send.at[k + 2], w_r.at[k + 2], dev(xpeers[d - 1], z, y, core))

    to_rows(g_e, t_e, 0)
    lo_ref[...] = rows[...].astype(BF).reshape(n, T, D)

    wait(dg.at[pl.ds(0, NZ - 1)], den_g)
    for h in range(HALVES):
        wait(zb2.at[h, pl.ds(1, NZ - 1)], zs_r.at[1, h])
        gd[0, x, h] = jnp.sum(zb2[h], axis=0)
        to_z(gd, h, 1)

    w_kv = jnp.concatenate([wk_ref[...], wv_ref[...]], axis=1)
    minus = jnp.full((n, D), -1.0, BF)

    def third_loop(chunk, _):
        gathered(chunk, gd, 1)
        ps = [chunk * GROUP + j for j in range(GROUP)]
        owns = [slice(j * n, (j + 1) * n) for j in range(GROUP)]
        wps, us, dvs = [], [], []
        for p in ps:
            dsum = gd[p].reshape(K, D)
            d_b = dsum.astype(BF)
            both = jnp.concatenate([d_b, (dsum * gs[p].reshape(K, D)).astype(BF)], axis=1)
            wp = wexp[p] * (1.0 / dg[p][:, 0:K])
            wps.append(wp)
            us.append(mm_nt(jnp.concatenate([vals[p], minus], axis=1), both))
            dvs.append(mm(wp.astype(BF), d_b).astype(BF))
        ds_b = (c * (stack(wps) * stack(us))).astype(BF)
        ku = stack([kunit[p] for p in ps])
        rk = stack([kscale[p] for p in ps])
        h = stack([hid[p] for p in ps])
        dku = mm(ds_b, pu_b)
        dk = (rk * (dku - ku * means(dku * ku))).astype(BF)
        dkv = jnp.concatenate([dk, stack(dvs)], axis=1)
        acc_p[...] += mm_tn(ds_b, ku.astype(BF))
        acc_kv[...] += mm_tn(h, dkv)
        dh = mm_nt(dkv, w_kv)
        for j, p in enumerate(ps):
            t = step_at(chunk, j)
            rows[pl.ds(t, n, stride=T), :] = mm(mask_of(t), (pre[p] + dh[owns[j]]).astype(BF))
        return 0

    gather(gd, 1)
    along_z(t_e, z_e, 0)
    lax.fori_loop(0, chunks, third_loop, 0)

    g_l[:, 0:half] = acc_kv[:, 0:D].reshape(R, half, RX, D)
    g_l[:, half:NX] = acc_kv[:, D:2 * D].reshape(R, half, RX, D)
    g_p[...] = acc_p[...].reshape(R, RP, D)
    for dr in range(R):
        pr = lax.rem(r + dr, R)
        px = lax.rem(pr, NX)
        dx = lax.rem(px - x + NX, NX)
        if dr:
            start(g_p.at[pr], t_p.at[dr * NX + dx], w_send.at[6], w_r.at[6], dev_r(px, pr))
        else:
            @pl.when(dx == 0)
            def _():
                t_p[0] = g_p[r]

            @pl.when(dx != 0)
            def _():
                start(g_p.at[r], t_p.at[dx], w_send.at[9], w_r.at[6], dev_r(px, r))
    to_rows(g_l, t_l, 3)
    meets = x == lax.rem(r, NX)
    along_x(z_e, f_e, 0)
    gi_ref[...] = rows[...].astype(BF).reshape(n, T, D)
    wait(t_l.at[pl.ds(1, R * NX - 1)], w_r.at[3])
    z_l[z] = jnp.sum(t_l[...], axis=0)

    def late_z(both):
        for d in far_z:
            device = dev(x, zpeers[d - 1], y, core)
            start(z_l.at[z], z_l.at[z], w_send.at[4], w_r.at[4], device)
            if both:
                start(z_p.at[z], z_p.at[z], w_send.at[7], w_r.at[7], device)

    @pl.when(meets)
    def _():
        wait(t_p.at[pl.ds(1, R * NX - 1)], w_r.at[6])
        z_p[z] = jnp.sum(t_p[...], axis=0)
        late_z(True)

    @pl.when(jnp.logical_not(meets))
    def _():
        late_z(False)

    along_x(z_l, f_l, 3)

    @pl.when(meets)
    def _():
        wait(z_p.at[pl.ds(0, NZ - 1)], w_r.at[7])
        dpu = jnp.sum(z_p[...], axis=0)
        prow = proj_ref[pl.ds(pl.multiple_of(r * RP, RP), RP), :]
        rp = row_scale(prow)
        pun = prow * rp
        f_p[...] = rp * (dpu - pun * row_mean(dpu * pun))
        for d in far_x:
            start(f_p, f_p, w_send.at[8], w_r.at[8], dev(xpeers[d - 1], z, y, core))

    wait(f_e.at[pl.ds(0, NX - 1)], w_r.at[2])
    final = f_e[...].reshape(2 * RG, D)
    gq_ref[...] = final[0:RG]
    go_ref[...] = final[RG:2 * RG]
    wait(f_l.at[pl.ds(0, NX - 1)], w_r.at[5])
    final = f_l[...].reshape(2 * RG, D)
    gk_ref[...] = final[0:RG]
    gv_ref[...] = final[RG:2 * RG]

    @pl.when(jnp.logical_not(meets))
    def _():
        wait(f_p, w_r.at[8])

    gp_ref[...] = f_p[...]

    wait(xb1, send.at[0])
    wait(zb1.at[:, pl.ds(1, NZ - 1)], send.at[1])
    wait(xb2, send.at[2])
    wait(zb2.at[:, pl.ds(1, NZ - 1)], send.at[3])
    wait(xb1, send.at[4])
    wait(zb1.at[:, pl.ds(1, NZ - 1)], send.at[5])
    wait(xb2, send.at[6])
    wait(zb2.at[:, pl.ds(1, NZ - 1)], send.at[7])
    wait(db, send.at[8])
    wait(dzb.at[pl.ds(1, NZ - 1)], send.at[9])
    wait(dzb.at[pl.ds(1, NZ - 1)], send.at[10])
    for k, t_buf, z_buf, f_buf in ((0, t_e, z_e, f_e), (3, t_l, z_l, f_l)):
        wait(t_buf.at[pl.ds(1, R * NX - 1)], w_send.at[k])
        wait(z_buf.at[pl.ds(0, NZ - 1)], w_send.at[k + 1])
        wait(f_buf.at[pl.ds(0, NX - 1)], w_send.at[k + 2])
    wait(g_p.at[pl.ds(0, R - 1)], w_send.at[6])

    @pl.when(jnp.logical_not(meets))
    def _():
        wait(f_p, w_send.at[9])

    @pl.when(meets)
    def _():
        wait(z_p.at[pl.ds(0, NZ - 1)], w_send.at[7])
        wait(t_p.at[pl.ds(0, NX - 1)], w_send.at[8])


def hand_out(*refs):
    sem = refs[-1]
    copies = [pltpu.make_async_copy(refs[i], refs[i + 7], sem.at[i]) for i in range(7)]
    for copy in copies:
        copy.start()
    for copy in copies:
        copy.wait()


def per_device(dims, inputs, mask, projector, w_key, w_value, w_query, w_out, cotangent):
    NX, NZ, NY, NC, n, T, K, D = dims
    R = NY * NC
    KH = K // NX // HALVES
    RG, RP = D // R, K // R
    RX = 2 * RG // NX
    hbm = pl.BlockSpec(memory_space=pltpu.HBM)
    vm = pl.BlockSpec(memory_space=pltpu.VMEM)
    steps = jax.ShapeDtypeStruct((n, T, D), BF)
    part = jax.ShapeDtypeStruct((RG, D), F32)
    operands = [
        pltpu.with_memory_space_constraint(a, pltpu.HBM)
        for a in (inputs, jnp.swapaxes(mask, 0, 1), projector, w_key, w_value, w_query, w_out, cotangent)
    ]
    lo, gi, gp, gk, gv, gq, go = pl.pallas_call(
        functools.partial(kernel, dims),
        out_shape=(steps, steps, jax.ShapeDtypeStruct((RP, D), F32), part, part, part, part),
        in_specs=[hbm] * 8,
        out_specs=(vm,) * 7,
        scratch_shapes=[
            pltpu.VMEM((n, T, D), BF),
            pltpu.VMEM((T, n), jnp.int32),
            pltpu.VMEM((K, D), F32),
            pltpu.VMEM((D, D), BF),
            pltpu.VMEM((D, D), BF),
            pltpu.VMEM((D, D), BF),
            pltpu.VMEM((D, D), BF),
            pltpu.VMEM((n, T, D), BF),
            pltpu.VMEM((n * T, D), F32),
            pltpu.VMEM((T, n, D), BF),
            pltpu.VMEM((T, n, D), F32),
            pltpu.VMEM((T, n, D), F32),
            pltpu.VMEM((T, n, D), BF),
            pltpu.VMEM((T, n, D), F32),
            pltpu.VMEM((T, n, D), F32),
            pltpu.VMEM((T, n, D), BF),
            pltpu.VMEM((T, n, D), BF),
            pltpu.VMEM((T, n, K), F32),
            pltpu.VMEM((T, n, D), F32),
            pltpu.VMEM((T, n, D), BF),
            pltpu.VMEM((T, n, K), BF),
            pltpu.VMEM((T, K, D), BF),
            pltpu.VMEM((T, NX, HALVES, KH, D), F32),
            pltpu.VMEM((T, HALVES, NX - 1, KH, D), F32),
            pltpu.VMEM((T, HALVES, KH, D), F32),
            pltpu.VMEM((HALVES, NZ, KH, D), F32),
            pltpu.VMEM((T, NX, HALVES, KH, D), F32),
            pltpu.VMEM((T, NX, HALVES, KH, D), F32),
            pltpu.VMEM((T, HALVES, NX - 1, KH, D), F32),
            pltpu.VMEM((T, HALVES, KH, D), F32),
            pltpu.VMEM((HALVES, NZ, KH, D), F32),
            pltpu.VMEM((T, NX, HALVES, KH, D), F32),
            pltpu.VMEM((T, 1, D), F32),
            pltpu.VMEM((NX - 1, T, 1, D), F32),
            pltpu.VMEM((T, 1, D), F32),
            pltpu.VMEM((NZ, 1, D), F32),
            pltpu.VMEM((T, 1, D), F32),
            pltpu.VMEM((K, D), F32),
            pltpu.VMEM((D, 2 * D), F32),
            pltpu.VMEM((D, D), F32),
            pltpu.VMEM((D, D), F32),
            pltpu.VMEM((R, NX, RX, D), F32),
            pltpu.VMEM((R * NX, RX, D), F32),
            pltpu.VMEM((NZ, RX, D), F32),
            pltpu.VMEM((NX, RX, D), F32),
            pltpu.VMEM((R, NX, RX, D), F32),
            pltpu.VMEM((R * NX, RX, D), F32),
            pltpu.VMEM((NZ, RX, D), F32),
            pltpu.VMEM((NX, RX, D), F32),
            pltpu.VMEM((R, RP, D), F32),
            pltpu.VMEM((R * NX, RP, D), F32),
            pltpu.VMEM((NZ, RP, D), F32),
            pltpu.VMEM((RP, D), F32),
            pltpu.SemaphoreType.DMA((8,)),
            pltpu.SemaphoreType.DMA((2, HALVES, T // SENT)),
            pltpu.SemaphoreType.DMA((2, HALVES)),
            pltpu.SemaphoreType.DMA((2, HALVES, T // SENT)),
            pltpu.SemaphoreType.DMA((2, HALVES, T // SENT)),
            pltpu.SemaphoreType.DMA((T // GROUP,)),
            pltpu.SemaphoreType.DMA,
            pltpu.SemaphoreType.DMA,
            pltpu.SemaphoreType.DMA((9,)),
            pltpu.SemaphoreType.DMA((11,)),
            pltpu.SemaphoreType.DMA((10,)),
        ],
        compiler_params=pltpu.CompilerParams(
            collective_id=0, has_side_effects=True, vmem_limit_bytes=48 << 20
        ),
    )(*operands)
    return tuple(
        pl.pallas_call(
            hand_out,
            out_shape=tuple(jax.ShapeDtypeStruct(a.shape, a.dtype) for a in (lo, gi, gp, gk, gv, gq, go)),
            in_specs=[vm] * 7,
            out_specs=(hbm,) * 7,
            scratch_shapes=[pltpu.SemaphoreType.DMA((7,))],
            compiler_params=pltpu.CompilerParams(vmem_limit_bytes=4 << 20),
        )(lo, gi, gp, gk, gv, gq, go)
    )


def build(torus, n, T, K, D):
    dims = tuple(torus.shape[a] for a in AXES) + (n, T, K, D)
    in_specs = (P(SENSOR, TIME, None), P(SENSOR, TIME), P(), P(), P(), P(), P(), P(SENSOR, TIME, None))
    rows = P(TIME, None)
    out_specs = (P(SENSOR, TIME, None), P(SENSOR, TIME, None), rows, rows, rows, rows, rows)
    return jax.shard_map(
        functools.partial(per_device, dims), mesh=torus, in_specs=in_specs, out_specs=out_specs, check_vma=False
    )


def solution(mesh):
    torus = Mesh(mesh.devices.reshape(4, 16, 4, 2), AXES)
    return build(torus, 4096 // 64, 128 // 8, 64, 128)
```

```python
import functools

import jax
import jax.numpy as jnp
from jax import lax
from jax.experimental import pallas as pl
from jax.experimental.pallas import tpu as pltpu
from jax.sharding import Mesh
from jax.sharding import PartitionSpec as P

AXES = ("sx", "sz", "ty", "tc")
SENSOR = ("sx", "sz")
TIME = ("ty", "tc")
MESH_ID = pl.DeviceIdType.MESH
SHARPNESS = 12.0
EPS = 1e-06
GROUP = 4
SENT = 4
HALVES = 2
BF = jnp.bfloat16
F32 = jnp.float32


def mm(a, b):
    return lax.dot_general(a, b, (((1,), (0,)), ((), ())), preferred_element_type=F32)


def mm_nt(a, b):
    return lax.dot_general(a, b, (((1,), (1,)), ((), ())), preferred_element_type=F32)


def mm_tn(a, b):
    return lax.dot_general(a, b, (((0,), (0,)), ((), ())), preferred_element_type=F32)


def row_scale(v):
    return lax.rsqrt(jnp.mean(v * v, axis=-1, keepdims=True) + EPS)


def row_mean(v):
    return jnp.mean(v, axis=-1, keepdims=True)


def stack(parts):
    return jnp.concatenate(parts, axis=0)


def kernel(
    dims,
    x_hbm, mask_hbm, proj_hbm, wk_hbm, wv_hbm, wq_hbm, wo_hbm, cot_hbm,
    lo_ref, gi_ref, gp_ref, gk_ref, gv_ref, gq_ref, go_ref,
    x_ref, mask_ref, proj_ref, wk_ref, wv_ref, wq_ref, wo_ref, cot_ref,
    rows, hid, kunit, kscale, vals, qunit, qscale, cott, dnorm, wexp, pre, norm, dsoft, sunit,
    num1, xb1, zs1, zb1, gs,
    num2, xb2, zs2, zb2, gd,
    dn, db, dz, dzb, dg,
    acc_p, acc_kv, acc_q, acc_o,
    g_e, t_e, z_e, f_e, g_l, t_l, z_l, f_l, g_p, t_p, z_p, f_p,
    in_s, xs_r, zs_r, ag_r, xag_r, den_r, den_z, den_g, w_r, send, w_send,
):
    NX, NZ, NY, NC, n, T, K, D = dims
    KC = K // NX
    KH = KC // HALVES
    R = NY * NC
    RG, RP = D // R, K // R
    RX = 2 * RG // NX
    c = SHARPNESS / D
    x, z, y, core = [lax.axis_index(a) for a in AXES]
    r = y * NC + core

    def dev(ax, az, ay, ac):
        return (ax, az, ay, ac)

    def dev_r(ax, p):
        return (ax, z, lax.div(p, NC), lax.rem(p, NC))

    xpeers = [lax.rem(x + d, NX) for d in range(1, NX)]
    zpeers = [lax.rem(z + d, NZ) for d in range(1, NZ)]
    far_x = sorted(range(1, NX), key=lambda d: -min(d, NX - d))
    far_z = sorted(range(1, NZ), key=lambda d: -min(d, NZ - d))
    plane = [(dr, dx) for dr in range(R) for dx in range(NX) if dr or dx]
    plane.sort(key=lambda o: -(min(o[0], R - o[0]) + NC * min(o[1], NX - o[1])))

    loads = [
        pltpu.make_async_copy(a, b, in_s.at[i])
        for i, (a, b) in enumerate([
            (x_hbm, x_ref), (mask_hbm, mask_ref), (proj_hbm, proj_ref), (wk_hbm, wk_ref), (wv_hbm, wv_ref),
            (wq_hbm, wq_ref), (wo_hbm, wo_ref), (cot_hbm, cot_ref),
        ])
    ]
    for load in loads:
        load.start()

    barrier = pltpu.get_barrier_semaphore()
    for p in zpeers:
        pl.semaphore_signal(barrier, inc=1, device_id=dev(x, p, y, core), device_id_type=MESH_ID)
    for dr, dx in plane:
        pl.semaphore_signal(
            barrier, inc=1, device_id=dev_r(lax.rem(x + dx, NX), lax.rem(r + dr, R)), device_id_type=MESH_ID
        )

    def start(src, dst, s_sem, r_sem, device):
        pltpu.make_async_remote_copy(
            src_ref=src, dst_ref=dst, send_sem=s_sem, recv_sem=r_sem, device_id=device, device_id_type=MESH_ID
        ).start()

    def wait(ref, sem):
        pltpu.make_async_copy(ref, ref, sem).wait()

    def step_at(chunk, j):
        ahead = GROUP // 2 * chunk + (j + 1) // 2
        return lax.rem(z + (T - ahead if j % 2 else ahead), T)

    def position(off):
        return 2 * off if off < T - off else 2 * (T - off) - 1

    chunks = T // GROUP
    ones = jnp.ones((D, D), BF)
    diagonal = lax.broadcasted_iota(jnp.int32, (n, n), 0) == lax.broadcasted_iota(jnp.int32, (n, n), 1)

    def mask_of(t):
        return jnp.where(diagonal, mask_ref[pl.ds(t, 1), :].astype(F32), 0.0).astype(BF)

    def means(v):
        return mm(v.astype(BF), ones) * (1.0 / D)

    dn[...] = jnp.zeros_like(dn)
    for load in loads[:6]:
        load.wait()
    proj = proj_ref[...]
    punit = proj * row_scale(proj)
    pu_b = punit.astype(BF)

    rows[...] = x_ref[...].reshape(n * T, D).astype(F32)

    def send_columns(g, h, num, xb, phase):
        some = pl.ds(g * SENT, SENT)
        for d in far_x:
            start(num.at[some, xpeers[d - 1], h], xb.at[some, h, d - 1], send.at[2 * phase], xs_r.at[phase, h, g],
                  dev(xpeers[d - 1], z, y, core))

    def to_owner(g, h, num, xb, zs, zb, phase):
        wait(xb.at[pl.ds(g * SENT, SENT), h], xs_r.at[phase, h, g])
        for k in range(SENT):
            at = g * SENT + k
            total = num[at, x, h]
            for d in range(1, NX):
                total = total + xb[at, h, d - 1]
            if at == 0:
                zb[h, 0] = total
            else:
                zs[at, h] = total
                off = T - (at + 1) // 2 if at % 2 else at // 2
                start(zs.at[at, h], zb.at[h, off], send.at[2 * phase + 1], zs_r.at[phase, h],
                      dev(x, zpeers[off - 1], y, core))

    def den_to_owner(chunk):
        mine = pl.ds(chunk * GROUP, GROUP)
        wait(db.at[pl.ds(0, NX - 1), mine], den_r.at[chunk])
        total = dn[mine]
        for d in range(1, NX):
            total = total + db[d - 1, mine]
        dz[mine] = total
        for j in range(GROUP):
            at = chunk * GROUP + j
            off = T - (at + 1) // 2 if at % 2 else at // 2
            if at == 0:
                dzb[0] = total[0]
            else:
                start(dz.at[at], dzb.at[off], send.at[9], den_z, dev(x, zpeers[off - 1], y, core))

    def to_z(g, h, phase):
        for d in far_z:
            at = position(NZ - d)
            start(g.at[0, x, h], g.at[at, x, h], send.at[5 + 2 * phase], ag_r.at[phase, h, at // SENT],
                  dev(x, zpeers[d - 1], y, core))

    def forward(k, h, g, phase):
        some = pl.ds(k * SENT, SENT)
        came = some if k else pl.ds(1, SENT - 1)
        wait(g.at[came, x, h], ag_r.at[phase, h, k])
        for d in far_x:
            start(g.at[some, x, h], g.at[some, x, h], send.at[4 + 2 * phase], xag_r.at[phase, h, k],
                  dev(xpeers[d - 1], z, y, core))

    def gather(g, phase):
        units = [(k, h) for h in range(HALVES) for k in range(T // SENT)]
        if phase == 0:
            units.sort(key=lambda u: (u[1], -u[0]))
        for k, h in units:
            forward(k, h, g, phase)

    def gathered(chunk, g, phase):
        for k in range(GROUP // SENT):
            p = chunk * (GROUP // SENT) + k
            for h in range(HALVES):
                wait(g.at[pl.ds(p * SENT, SENT), pl.ds(0, NX - 1), h], xag_r.at[phase, h, p])

    per_chunk = GROUP // SENT

    def first_loop(step, _):
        chunk = chunks - 1 - step
        ts = [step_at(chunk, j) for j in range(GROUP)]
        hs = []
        for j, t in enumerate(ts):
            hs.append(mm(mask_of(t), rows[pl.ds(t, n, stride=T), :].astype(BF)).astype(BF))
        h = stack(hs)
        kr = mm(h, wk_ref[...])
        rk = lax.rsqrt(means(kr * kr) + EPS)
        ku = kr * rk
        v = mm(h, wv_ref[...]).astype(BF)
        w = jnp.exp(c * mm_nt(ku.astype(BF), pu_b))
        wb = w.astype(BF)
        for j in range(GROUP):
            own = slice(j * n, (j + 1) * n)
            p = chunk * GROUP + j
            num1[p] = mm_tn(wb[own], v[own]).reshape(NX, HALVES, KH, D)
            dn[p, :, 0:K] = jnp.sum(w[own], axis=0, keepdims=True)
            hid[p] = h[own]
            kunit[p] = ku[own]
            kscale[p] = rk[own]
            vals[p] = v[own]
            wexp[p] = w[own]

        @pl.when(step == 0)
        def _():
            pl.semaphore_wait(barrier, NZ - 1 + R * NX - 1)

        mine = pl.ds(chunk * GROUP, GROUP)
        for d in far_x:
            start(dn.at[mine], db.at[d - 1, mine], send.at[8], den_r.at[chunk], dev(xpeers[d - 1], z, y, core))
        for k in reversed(range(per_chunk)):
            send_columns(chunk * per_chunk + k, 0, num1, xb1, 0)
        return 0

    lax.fori_loop(0, chunks, first_loop, 0)
    for h in range(1, HALVES):
        for g in reversed(range(T // SENT)):
            send_columns(g, h, num1, xb1, 0)

    loads[6].wait()
    loads[7].wait()
    rows[...] = cot_ref[...].reshape(n * T, D).astype(F32)

    def cot_loop(chunk, _):
        cs = []
        for j in range(GROUP):
            cs.append(rows[pl.ds(step_at(chunk, j), n, stride=T), :].astype(BF))
        d = mm_nt(stack(cs), wo_ref[...]).astype(BF)
        qr = mm(stack([hid[chunk * GROUP + j] for j in range(GROUP)]), wq_ref[...])
        rq = lax.rsqrt(means(qr * qr) + EPS)
        qu = qr * rq
        for j in range(GROUP):
            own = slice(j * n, (j + 1) * n)
            p = chunk * GROUP + j
            cott[p] = cs[j]
            dnorm[p] = d[own]
            qscale[p] = rq[own]
            qunit[p] = qu[own]
        return 0

    lax.fori_loop(0, chunks // 2, cot_loop, 0)
    for chunk in reversed(range(chunks)):
        den_to_owner(chunk)
        for g in reversed(range(chunk * per_chunk, (chunk + 1) * per_chunk)):
            to_owner(g, 0, num1, xb1, zs1, zb1, 0)
    lax.fori_loop(chunks // 2, chunks, cot_loop, 0)
    for h in range(1, HALVES):
        for g in reversed(range(T // SENT)):
            to_owner(g, h, num1, xb1, zs1, zb1, 0)

    wait(dzb.at[pl.ds(1, NZ - 1)], den_z)
    den_row = jnp.sum(dzb[...], axis=0)
    dg[0] = den_row
    at = lax.broadcasted_iota(jnp.int32, (KC, D), 1) == lax.broadcasted_iota(jnp.int32, (KC, D), 0) + x * KC
    den_col = jnp.sum(jnp.where(at, den_row, 0.0), axis=1, keepdims=True)
    for h in range(HALVES):
        wait(zb1.at[h, pl.ds(1, NZ - 1)], zs_r.at[0, h])
        gs[0, x, h] = jnp.sum(zb1[h], axis=0) / den_col[h * KH:(h + 1) * KH]
        to_z(gs, h, 0)
    for d in far_z:
        start(dg.at[0], dg.at[position(NZ - d)], send.at[10], den_g, dev(x, zpeers[d - 1], y, core))

    acc_q[...] = jnp.zeros_like(acc_q)
    acc_o[...] = jnp.zeros_like(acc_o)
    acc_kv[...] = jnp.zeros_like(acc_kv)
    acc_p[...] = jnp.zeros_like(acc_p)

    def second_loop(step, _):
        chunk = chunks - 1 - step
        gathered(chunk, gs, 0)
        ps = [chunk * GROUP + j for j in range(GROUP)]
        owns = [slice(j * n, (j + 1) * n) for j in range(GROUP)]
        keys = [slice(j * K, (j + 1) * K) for j in range(GROUP)]
        s = stack([gs[p].reshape(K, D) for p in ps])
        s_b = s.astype(BF)
        rs = lax.rsqrt(means(s * s) + EPS)
        su = s * rs
        su_b = su.astype(BF)
        qu = stack([qunit[p] for p in ps])
        qu_b = qu.astype(BF)
        e = jnp.exp(c * stack([mm_nt(qu_b[o], su_b[k]) for o, k in zip(owns, keys)]))
        e_b = e.astype(BF)
        mixed = stack([mm(e_b[o], s_b[k]) for o, k in zip(owns, keys)])
        inv = 1.0 / mm(e_b, ones[0:K])
        dy = stack([dnorm[p] for p in ps]).astype(F32)
        rb = lax.rsqrt(means(mixed * mixed) * (inv * inv) + EPS)
        scale = rb * inv
        bn = mixed * scale
        normed = bn.astype(BF)
        dbl_b = (rb * (dy - bn * (scale * means(dy * mixed)))).astype(BF)
        a = e * inv[:, 0:K]
        a_b = a.astype(BF)
        ada = a * stack([mm_nt(dbl_b[o], s_b[k]) for o, k in zip(owns, keys)])
        ds_b = (c * (ada - a * mm(ada.astype(BF), ones[0:K, 0:K]))).astype(BF)
        dsu = stack([mm_tn(ds_b[o], qu_b[o]) for o in owns])
        dsum = stack([mm_tn(a_b[o], dbl_b[o]) for o in owns])
        dsum = dsum + rs * (dsu - su * means(dsu * su))
        for j, p in enumerate(ps):
            num2[p] = dsum[keys[j]].reshape(NX, HALVES, KH, D)
        for h in range(HALVES):
            for k in range(per_chunk):
                send_columns(chunk * per_chunk + k, h, num2, xb2, 1)
        for j, p in enumerate(ps):
            norm[p] = normed[owns[j]]
            dsoft[p] = ds_b[owns[j]]
            sunit[p] = su_b[keys[j]]
        return 0

    def second_rest(chunk):
        ps = [chunk * GROUP + j for j in range(GROUP)]
        owns = [slice(j * n, (j + 1) * n) for j in range(GROUP)]
        normed = stack([norm[p] for p in ps])
        qu = stack([qunit[p] for p in ps])
        rq = stack([qscale[p] for p in ps])
        dqu = stack([mm(dsoft[p], sunit[p]) for p in ps])
        dq = (rq * (dqu - qu * means(dqu * qu))).astype(BF)
        h = stack([hid[p] for p in ps])
        ct = stack([cott[p] for p in ps])
        lo = h.astype(F32) + mm(normed, wo_ref[...])
        part = ct.astype(F32) + mm_nt(dq, wq_ref[...])
        acc_o[...] += mm_tn(normed, ct)
        acc_q[...] += mm_tn(h, dq)
        for j, p in enumerate(ps):
            rows[pl.ds(step_at(chunk, j), n, stride=T), :] = lo[owns[j]]
            pre[p] = part[owns[j]]

    def second_owner(chunk):
        for h in range(HALVES):
            for k in range(per_chunk):
                to_owner(chunk * per_chunk + k, h, num2, xb2, zs2, zb2, 1)

    gather(gs, 0)
    lax.fori_loop(0, chunks, second_loop, 0)
    late = chunks // 2
    for chunk in reversed(range(late, chunks)):
        second_rest(chunk)
    for chunk in reversed(range(chunks)):
        second_owner(chunk)
    for chunk in reversed(range(late)):
        second_rest(chunk)

    half = NX // 2
    g_e[:, 0:half] = acc_q[...].reshape(R, half, RX, D)
    g_e[:, half:NX] = acc_o[...].reshape(R, half, RX, D)

    def to_rows(g, t_buf, k):
        for dr, dx in plane:
            px, pr = lax.rem(x + dx, NX), lax.rem(r + dr, R)
            start(g.at[pr, px], t_buf.at[dr * NX + dx], w_send.at[k], w_r.at[k], dev_r(px, pr))
        t_buf[0] = g[r, x]

    def along_z(t_buf, z_buf, k):
        wait(t_buf.at[pl.ds(1, R * NX - 1)], w_r.at[k])
        z_buf[z] = jnp.sum(t_buf[...], axis=0)
        for d in far_z:
            start(z_buf.at[z], z_buf.at[z], w_send.at[k + 1], w_r.at[k + 1], dev(x, zpeers[d - 1], y, core))

    def along_x(z_buf, f_buf, k):
        wait(z_buf.at[pl.ds(0, NZ - 1)], w_r.at[k + 1])
        f_buf[x] = jnp.sum(z_buf[...], axis=0)
        for d in far_x:
            start(f_buf.at[x], f_buf.at[x], w_send.at[k + 2], w_r.at[k + 2], dev(xpeers[d - 1], z, y, core))

    to_rows(g_e, t_e, 0)
    lo_ref[...] = rows[...].astype(BF).reshape(n, T, D)

    wait(dg.at[pl.ds(0, NZ - 1)], den_g)
    for h in range(HALVES):
        wait(zb2.at[h, pl.ds(1, NZ - 1)], zs_r.at[1, h])
        gd[0, x, h] = jnp.sum(zb2[h], axis=0)
        to_z(gd, h, 1)

    w_kv = jnp.concatenate([wk_ref[...], wv_ref[...]], axis=1)
    minus = jnp.full((n, D), -1.0, BF)

    def third_loop(chunk, _):
        gathered(chunk, gd, 1)
        ps = [chunk * GROUP + j for j in range(GROUP)]
        owns = [slice(j * n, (j + 1) * n) for j in range(GROUP)]
        wps, us, dvs = [], [], []
        for p in ps:
            dsum = gd[p].reshape(K, D)
            d_b = dsum.astype(BF)
            both = jnp.concatenate([d_b, (dsum * gs[p].reshape(K, D)).astype(BF)], axis=1)
            wp = wexp[p] * (1.0 / dg[p][:, 0:K])
            wps.append(wp)
            us.append(mm_nt(jnp.concatenate([vals[p], minus], axis=1), both))
            dvs.append(mm(wp.astype(BF), d_b).astype(BF))
        ds_b = (c * (stack(wps) * stack(us))).astype(BF)
        ku = stack([kunit[p] for p in ps])
        rk = stack([kscale[p] for p in ps])
        h = stack([hid[p] for p in ps])
        dku = mm(ds_b, pu_b)
        dk = (rk * (dku - ku * means(dku * ku))).astype(BF)
        dkv = jnp.concatenate([dk, stack(dvs)], axis=1)
        acc_p[...] += mm_tn(ds_b, ku.astype(BF))
        acc_kv[...] += mm_tn(h, dkv)
        dh = mm_nt(dkv, w_kv)
        for j, p in enumerate(ps):
            t = step_at(chunk, j)
            rows[pl.ds(t, n, stride=T), :] = mm(mask_of(t), (pre[p] + dh[owns[j]]).astype(BF))
        return 0

    gather(gd, 1)
    along_z(t_e, z_e, 0)
    lax.fori_loop(0, chunks, third_loop, 0)

    g_l[:, 0:half] = acc_kv[:, 0:D].reshape(R, half, RX, D)
    g_l[:, half:NX] = acc_kv[:, D:2 * D].reshape(R, half, RX, D)
    g_p[...] = acc_p[...].reshape(R, RP, D)
    for dr in range(R):
        pr = lax.rem(r + dr, R)
        px = lax.rem(pr, NX)
        dx = lax.rem(px - x + NX, NX)
        if dr:
            start(g_p.at[pr], t_p.at[dr * NX + dx], w_send.at[6], w_r.at[6], dev_r(px, pr))
        else:
            @pl.when(dx == 0)
            def _():
                t_p[0] = g_p[r]

            @pl.when(dx != 0)
            def _():
                start(g_p.at[r], t_p.at[dx], w_send.at[9], w_r.at[6], dev_r(px, r))
    to_rows(g_l, t_l, 3)
    meets = x == lax.rem(r, NX)
    along_x(z_e, f_e, 0)
    gi_ref[...] = rows[...].astype(BF).reshape(n, T, D)
    wait(t_l.at[pl.ds(1, R * NX - 1)], w_r.at[3])
    z_l[z] = jnp.sum(t_l[...], axis=0)

    def late_z(both):
        for d in far_z:
            device = dev(x, zpeers[d - 1], y, core)
            start(z_l.at[z], z_l.at[z], w_send.at[4], w_r.at[4], device)
            if both:
                start(z_p.at[z], z_p.at[z], w_send.at[7], w_r.at[7], device)

    @pl.when(meets)
    def _():
        wait(t_p.at[pl.ds(1, R * NX - 1)], w_r.at[6])
        z_p[z] = jnp.sum(t_p[...], axis=0)
        late_z(True)

    @pl.when(jnp.logical_not(meets))
    def _():
        late_z(False)

    along_x(z_l, f_l, 3)

    @pl.when(meets)
    def _():
        wait(z_p.at[pl.ds(0, NZ - 1)], w_r.at[7])
        dpu = jnp.sum(z_p[...], axis=0)
        prow = proj_ref[pl.ds(pl.multiple_of(r * RP, RP), RP), :]
        rp = row_scale(prow)
        pun = prow * rp
        f_p[...] = rp * (dpu - pun * row_mean(dpu * pun))
        for d in far_x:
            start(f_p, f_p, w_send.at[8], w_r.at[8], dev(xpeers[d - 1], z, y, core))

    wait(f_e.at[pl.ds(0, NX - 1)], w_r.at[2])
    final = f_e[...].reshape(2 * RG, D)
    gq_ref[...] = final[0:RG]
    go_ref[...] = final[RG:2 * RG]
    wait(f_l.at[pl.ds(0, NX - 1)], w_r.at[5])
    final = f_l[...].reshape(2 * RG, D)
    gk_ref[...] = final[0:RG]
    gv_ref[...] = final[RG:2 * RG]

    @pl.when(jnp.logical_not(meets))
    def _():
        wait(f_p, w_r.at[8])

    gp_ref[...] = f_p[...]

    wait(xb1, send.at[0])
    wait(zb1.at[:, pl.ds(1, NZ - 1)], send.at[1])
    wait(xb2, send.at[2])
    wait(zb2.at[:, pl.ds(1, NZ - 1)], send.at[3])
    wait(xb1, send.at[4])
    wait(zb1.at[:, pl.ds(1, NZ - 1)], send.at[5])
    wait(xb2, send.at[6])
    wait(zb2.at[:, pl.ds(1, NZ - 1)], send.at[7])
    wait(db, send.at[8])
    wait(dzb.at[pl.ds(1, NZ - 1)], send.at[9])
    wait(dzb.at[pl.ds(1, NZ - 1)], send.at[10])
    for k, t_buf, z_buf, f_buf in ((0, t_e, z_e, f_e), (3, t_l, z_l, f_l)):
        wait(t_buf.at[pl.ds(1, R * NX - 1)], w_send.at[k])
        wait(z_buf.at[pl.ds(0, NZ - 1)], w_send.at[k + 1])
        wait(f_buf.at[pl.ds(0, NX - 1)], w_send.at[k + 2])
    wait(g_p.at[pl.ds(0, R - 1)], w_send.at[6])

    @pl.when(jnp.logical_not(meets))
    def _():
        wait(f_p, w_send.at[9])

    @pl.when(meets)
    def _():
        wait(z_p.at[pl.ds(0, NZ - 1)], w_send.at[7])
        wait(t_p.at[pl.ds(0, NX - 1)], w_send.at[8])


def hand_out(*refs):
    sem = refs[-1]
    copies = [pltpu.make_async_copy(refs[i], refs[i + 7], sem.at[i]) for i in range(7)]
    for copy in copies:
        copy.start()
    for copy in copies:
        copy.wait()


def per_device(dims, inputs, mask, projector, w_key, w_value, w_query, w_out, cotangent):
    NX, NZ, NY, NC, n, T, K, D = dims
    R = NY * NC
    KH = K // NX // HALVES
    RG, RP = D // R, K // R
    RX = 2 * RG // NX
    hbm = pl.BlockSpec(memory_space=pltpu.HBM)
    vm = pl.BlockSpec(memory_space=pltpu.VMEM)
    steps = jax.ShapeDtypeStruct((n, T, D), BF)
    part = jax.ShapeDtypeStruct((RG, D), F32)
    operands = [
        pltpu.with_memory_space_constraint(a, pltpu.HBM)
        for a in (inputs, jnp.swapaxes(mask, 0, 1), projector, w_key, w_value, w_query, w_out, cotangent)
    ]
    lo, gi, gp, gk, gv, gq, go = pl.pallas_call(
        functools.partial(kernel, dims),
        out_shape=(steps, steps, jax.ShapeDtypeStruct((RP, D), F32), part, part, part, part),
        in_specs=[hbm] * 8,
        out_specs=(vm,) * 7,
        scratch_shapes=[
            pltpu.VMEM((n, T, D), BF),
            pltpu.VMEM((T, n), jnp.int32),
            pltpu.VMEM((K, D), F32),
            pltpu.VMEM((D, D), BF),
            pltpu.VMEM((D, D), BF),
            pltpu.VMEM((D, D), BF),
            pltpu.VMEM((D, D), BF),
            pltpu.VMEM((n, T, D), BF),
            pltpu.VMEM((n * T, D), F32),
            pltpu.VMEM((T, n, D), BF),
            pltpu.VMEM((T, n, D), F32),
            pltpu.VMEM((T, n, D), F32),
            pltpu.VMEM((T, n, D), BF),
            pltpu.VMEM((T, n, D), F32),
            pltpu.VMEM((T, n, D), F32),
            pltpu.VMEM((T, n, D), BF),
            pltpu.VMEM((T, n, D), BF),
            pltpu.VMEM((T, n, K), F32),
            pltpu.VMEM((T, n, D), F32),
            pltpu.VMEM((T, n, D), BF),
            pltpu.VMEM((T, n, K), BF),
            pltpu.VMEM((T, K, D), BF),
            pltpu.VMEM((T, NX, HALVES, KH, D), F32),
            pltpu.VMEM((T, HALVES, NX - 1, KH, D), F32),
            pltpu.VMEM((T, HALVES, KH, D), F32),
            pltpu.VMEM((HALVES, NZ, KH, D), F32),
            pltpu.VMEM((T, NX, HALVES, KH, D), F32),
            pltpu.VMEM((T, NX, HALVES, KH, D), F32),
            pltpu.VMEM((T, HALVES, NX - 1, KH, D), F32),
            pltpu.VMEM((T, HALVES, KH, D), F32),
            pltpu.VMEM((HALVES, NZ, KH, D), F32),
            pltpu.VMEM((T, NX, HALVES, KH, D), F32),
            pltpu.VMEM((T, 1, D), F32),
            pltpu.VMEM((NX - 1, T, 1, D), F32),
            pltpu.VMEM((T, 1, D), F32),
            pltpu.VMEM((NZ, 1, D), F32),
            pltpu.VMEM((T, 1, D), F32),
            pltpu.VMEM((K, D), F32),
            pltpu.VMEM((D, 2 * D), F32),
            pltpu.VMEM((D, D), F32),
            pltpu.VMEM((D, D), F32),
            pltpu.VMEM((R, NX, RX, D), F32),
            pltpu.VMEM((R * NX, RX, D), F32),
            pltpu.VMEM((NZ, RX, D), F32),
            pltpu.VMEM((NX, RX, D), F32),
            pltpu.VMEM((R, NX, RX, D), F32),
            pltpu.VMEM((R * NX, RX, D), F32),
            pltpu.VMEM((NZ, RX, D), F32),
            pltpu.VMEM((NX, RX, D), F32),
            pltpu.VMEM((R, RP, D), F32),
            pltpu.VMEM((R * NX, RP, D), F32),
            pltpu.VMEM((NZ, RP, D), F32),
            pltpu.VMEM((RP, D), F32),
            pltpu.SemaphoreType.DMA((8,)),
            pltpu.SemaphoreType.DMA((2, HALVES, T // SENT)),
            pltpu.SemaphoreType.DMA((2, HALVES)),
            pltpu.SemaphoreType.DMA((2, HALVES, T // SENT)),
            pltpu.SemaphoreType.DMA((2, HALVES, T // SENT)),
            pltpu.SemaphoreType.DMA((T // GROUP,)),
            pltpu.SemaphoreType.DMA,
            pltpu.SemaphoreType.DMA,
            pltpu.SemaphoreType.DMA((9,)),
            pltpu.SemaphoreType.DMA((11,)),
            pltpu.SemaphoreType.DMA((10,)),
        ],
        compiler_params=pltpu.CompilerParams(
            collective_id=0, has_side_effects=True, vmem_limit_bytes=48 << 20
        ),
    )(*operands)
    return tuple(
        pl.pallas_call(
            hand_out,
            out_shape=tuple(jax.ShapeDtypeStruct(a.shape, a.dtype) for a in (lo, gi, gp, gk, gv, gq, go)),
            in_specs=[vm] * 7,
            out_specs=(hbm,) * 7,
            scratch_shapes=[pltpu.SemaphoreType.DMA((7,))],
            compiler_params=pltpu.CompilerParams(vmem_limit_bytes=4 << 20),
        )(lo, gi, gp, gk, gv, gq, go)
    )


def build(torus, n, T, K, D):
    dims = tuple(torus.shape[a] for a in AXES) + (n, T, K, D)
    in_specs = (P(SENSOR, TIME, None), P(SENSOR, TIME), P(), P(), P(), P(), P(), P(SENSOR, TIME, None))
    rows = P(TIME, None)
    out_specs = (P(SENSOR, TIME, None), P(SENSOR, TIME, None), rows, rows, rows, rows, rows)
    return jax.shard_map(
        functools.partial(per_device, dims), mesh=torus, in_specs=in_specs, out_specs=out_specs, check_vma=False
    )


def solution(mesh):
    torus = Mesh(mesh.devices.reshape(4, 16, 4, 2), AXES)
    return build(torus, 4096 // 64, 128 // 8, 64, 128)
```
